512 devices in a mesh: section: 2 (over x_hi), lat: 64 (over z, x_lo, core), tp: 4 (over y).
Axes of the slice: x: 4 (x_hi: 2, x_lo: 2; x = x_hi * 2 + x_lo), y: 4, z: 16, core: 2. Of those that a mesh axis runs over, the one named last changes fastest.
Arguments:
- initial_field: bfloat16 [2, 8, 192, 48, 192], P(None, 'tp', 'lat'), may hold values from -6 to 6
- first_gain: bfloat16 [2, 192], P('section'), may hold values from 0.25 to 1.75
- first_shift: bfloat16 [2, 192], P('section'), may hold values from -1.75 to 1.75
- qkv_weight: bfloat16 [2, 192, 576], P('section', None, 'tp'), may hold values from -0.4375 to 0.4375
- qkv_bias: bfloat16 [2, 576], P('section', 'tp'), may hold values from -1.75 to 1.75
- proj_weight: bfloat16 [2, 192, 192], P('section', None, 'tp'), may hold values from -0.4375 to 0.4375
- proj_bias: bfloat16 [2, 192], P('section', 'tp'), may hold values from -1.75 to 1.75
- second_gain: bfloat16 [2, 192], P('section'), may hold values from 0.25 to 1.75
- second_shift: bfloat16 [2, 192], P('section'), may hold values from -1.75 to 1.75
- expand_weight: bfloat16 [2, 192, 768], P('section', None, 'tp'), may hold values from -0.4375 to 0.4375
- expand_bias: bfloat16 [2, 768], P('section', 'tp'), may hold values from -1.75 to 1.75
- reduce_weight: bfloat16 [2, 768, 192], P('section', 'tp'), may hold values from -0.21875 to 0.21875
- reduce_bias: bfloat16 [2, 192], P('section', 'tp'), may hold values from -1.75 to 1.75
- earth_bias: float32 [2, 4, 64, 6, 1656], P('section', 'tp', 'lat'), may hold values from -4 to 340
Outputs:
- predicted_states: bfloat16 [2, 2, 8, 192, 48, 192], P('section', None, 'tp', 'lat')
The draws below stay inside these ranges and needn't reach their ends.
All inputs are finite; a program needn't handle non-finite values.
Results may differ from the reference program's by a relative error of at most 0.018.
Values may be sent and summed in bfloat16 or wider, within the bound.
No kernel may reach another device: no remote copies, remote signals or barrier semaphores. Data moves between devices by JAX's collectives and lax.ppermute only.
A program may use at most 64 MiB of HBM per device.

```python
import jax
import jax.numpy as jnp
import numpy as np
from jax import lax

C = 192
HEADS = 6
LEV = 8
LON = 48
MICRO = 2
WZ = 2
WH = 6
WW = 12
LAT = 192
MLP_WIDTH = 768
HALF_BIAS_COUNT = 1656


def draw_earth_bias(key, part):
    half_rows = WH // 2
    shape = (2, LEV // WZ, LAT // half_rows, HEADS, HALF_BIAS_COUNT)
    noise = jnp.clip(jax.random.normal(jax.random.fold_in(key, 11), shape, jnp.float32), -4.0, 4.0)
    return noise


def shard_levels(key, shape, cuts, smallest, largest):
    level = 1.0
    for dim, blocks in cuts:
        heights = jax.random.uniform(jax.random.fold_in(jax.random.fold_in(key, 6), dim), (blocks,), jnp.float32, smallest / len(cuts), largest / len(cuts))
        level = level * jnp.repeat(jnp.exp(heights), shape[dim] // blocks).reshape((-1,) + (1,) * (len(shape) - 1 - dim))
    return level


def centred(own_key, dims, scale, most, cuts=(), dtype=jnp.bfloat16):
    factor_of = shard_levels(own_key, dims, cuts, -0.22, 0.18) if cuts else 1.0
    values = jax.random.normal(own_key, dims, jnp.float32) * scale * factor_of
    return jnp.minimum(jnp.maximum(values, -most), most).astype(dtype)


def setup_inputs(seed: int = 0) -> dict:
    key_list = jax.random.split(jax.random.key(seed), 15)
    return {
        "initial_field": centred(key_list[0], (MICRO, LEV, LAT, LON, C), 1.0, 6.0, ((1, 4), (2, 64))),
        "first_gain": jnp.clip(1.0 + 0.15 * jax.random.normal(key_list[1], (2, C), jnp.float32), 0.25, 1.75).astype(jnp.bfloat16),
        "first_shift": centred(key_list[2], (2, C), 0.3, 1.75, ((0, 2),)),
        "qkv_weight": centred(key_list[3], (2, C, 3 * C), C ** -0.5, 0.4375, ((0, 2), (2, 4))),
        "qkv_bias": centred(key_list[4], (2, 3 * C), 0.3, 1.75, ((0, 2), (1, 4))),
        "proj_weight": centred(key_list[5], (2, C, C), C ** -0.5, 0.4375, ((0, 2), (2, 4))),
        "proj_bias": centred(key_list[6], (2, C), 0.3, 1.75, ((0, 2), (1, 4))),
        "second_gain": jnp.clip(1.0 + 0.15 * jax.random.normal(key_list[7], (2, C), jnp.float32), 0.25, 1.75).astype(jnp.bfloat16),
        "second_shift": centred(key_list[8], (2, C), 0.3, 1.75, ((0, 2),)),
        "expand_weight": centred(key_list[9], (2, C, MLP_WIDTH), C ** -0.5, 0.4375, ((0, 2), (2, 4))),
        "expand_bias": centred(key_list[10], (2, MLP_WIDTH), 0.3, 1.75, ((0, 2), (1, 4))),
        "reduce_weight": centred(key_list[11], (2, MLP_WIDTH, C), MLP_WIDTH ** -0.5, 0.21875, ((0, 2), (1, 4))),
        "reduce_bias": centred(key_list[12], (2, C), 0.3, 1.75, ((0, 2), (1, 4))),
        "earth_bias": draw_earth_bias(jax.random.fold_in(key_list[14], 71), 0),
    }


epsilon = 1e-05

def bias_entries():
    half_rows = WH // 2
    query_pos = np.arange(WZ * half_rows * WW)
    attended_location = np.arange(WZ * WH * WW)
    query_level = query_pos // (half_rows * WW)
    query_row = query_pos // WW % half_rows
    query_col = query_pos % WW
    key_level = attended_location // (WH * WW)
    key_row = attended_location // WW % WH
    key_column_index = attended_location % WW
    table_items = (((query_level[:, None] * WZ + key_level[None, :]) * half_rows + query_row[:, None]) * WH + key_row[None, :]) * (2 * WW - 1) + (query_col[:, None] - key_column_index[None, :] + WW - 1)
    return table_items.astype(np.int32)

def layer_norm(values, gain, offset):
    floats = values.astype(jnp.float32)
    middle_point = lax.optimization_barrier(jnp.mean(floats, axis=-1, keepdims=True))
    spread = lax.optimization_barrier(jnp.mean((floats - middle_point) ** 2, axis=-1, keepdims=True))
    return (floats - middle_point) * lax.rsqrt(spread + epsilon) * gain.astype(jnp.float32) + offset.astype(jnp.float32)

def to_windows(grid, band_rows):
    levels, lat_rows, lon_cols, feats = grid.shape
    shaped = grid.reshape(levels // WZ, WZ, lat_rows // band_rows, band_rows, lon_cols // WW, WW, feats)
    shaped = shaped.transpose(2, 0, 4, 1, 3, 5, 6)
    return shaped.reshape(lat_rows // band_rows, levels // WZ, lon_cols // WW, WZ * band_rows * WW, feats)

def from_windows(blocks, levels, lat_rows, lon_cols):
    band_rows = WH // 2
    feats = blocks.shape[-1]
    shaped = blocks.reshape(lat_rows // band_rows, levels // WZ, lon_cols // WW, WZ, band_rows, WW, feats)
    shaped = shaped.transpose(1, 3, 0, 4, 2, 5, 6)
    return shaped.reshape(levels, lat_rows, lon_cols, feats)

def earth_block(grid, model_index, params, bias_table):
    first_gain, first_shift, qkv_weight, qkv_bias, proj_weight, proj_bias, second_gain, second_shift, expand_weight, expand_bias, reduce_weight, reduce_bias = params
    levels, lat_rows, lon_cols, width = grid.shape
    heads = bias_table.shape[-2]
    head_size = width // heads
    scale = 1.0 / float(np.sqrt(head_size))
    normed = layer_norm(grid, first_gain[model_index], first_shift[model_index]).astype(jnp.bfloat16)
    flat = normed.reshape(-1, width)
    mixed = (jnp.dot(flat, qkv_weight[model_index], preferred_element_type=jnp.float32) + qkv_bias[model_index].astype(jnp.float32)).astype(jnp.bfloat16)
    mixed = mixed.reshape(levels, lat_rows, lon_cols, 3 * width)
    query_rows = to_windows(mixed[..., :width], WH // 2)
    keyvals = jnp.repeat(to_windows(mixed[..., width:], WH), 2, axis=0)
    table_items = jnp.asarray(bias_entries())
    tables = jnp.transpose(bias_table, (1, 0, 2, 3))

    def attend(pieces):
        query_block, keyval_block, table_block = pieces
        level_wins, meridian_slabs, query_count, feats = query_block.shape
        key_count = keyval_block.shape[2]
        bias_block = jnp.take(table_block, table_items, axis=2)
        query_heads = query_block.astype(jnp.float32).reshape(level_wins, meridian_slabs, query_count, heads, head_size)
        key_heads = keyval_block[..., :width].astype(jnp.float32).reshape(level_wins, meridian_slabs, key_count, heads, head_size)
        value_heads = keyval_block[..., width:].astype(jnp.float32).reshape(level_wins, meridian_slabs, key_count, heads, head_size)
        scores = jnp.einsum('lwqhd,lwkhd->lwhqk', query_heads, key_heads) * scale + bias_block[:, None]
        probs = jax.nn.softmax(scores, axis=-1).astype(jnp.bfloat16)
        attended = jnp.einsum('lwhqk,lwkhd->lwqhd', probs.astype(jnp.float32), value_heads)
        return attended.reshape(level_wins, meridian_slabs, query_count, width).astype(jnp.bfloat16)
    attended = lax.map(attend, (query_rows, keyvals, tables))
    merged = from_windows(attended, levels, lat_rows, lon_cols).reshape(-1, width)
    branch = jnp.dot(merged, proj_weight[model_index], preferred_element_type=jnp.float32) + proj_bias[model_index].astype(jnp.float32)
    middle = (grid.reshape(-1, width).astype(jnp.float32) + branch).astype(jnp.bfloat16)
    normed_two = layer_norm(middle, second_gain[model_index], second_shift[model_index]).astype(jnp.bfloat16)
    hidden = jax.nn.gelu(jnp.dot(normed_two, expand_weight[model_index], preferred_element_type=jnp.float32) + expand_bias[model_index].astype(jnp.float32), approximate=False).astype(jnp.bfloat16)
    result = (middle.astype(jnp.float32) + jnp.dot(hidden, reduce_weight[model_index], preferred_element_type=jnp.float32) + reduce_bias[model_index].astype(jnp.float32)).astype(jnp.bfloat16)
    return result.reshape(levels, lat_rows, lon_cols, width)

def reference(initial_field, first_gain, first_shift, qkv_weight, qkv_bias, proj_weight, proj_bias, second_gain, second_shift, expand_weight, expand_bias, reduce_weight, reduce_bias, earth_bias):
    params = (first_gain, first_shift, qkv_weight, qkv_bias, proj_weight, proj_bias, second_gain, second_shift, expand_weight, expand_bias, reduce_weight, reduce_bias)
    daily_lead_times = []
    quarter_lead_times = []
    for turn_index in range(MICRO):
        first_out = earth_block(initial_field[turn_index], 0, params, earth_bias[0])
        second_out = earth_block(first_out, 1, params, earth_bias[1])
        daily_lead_times.append(first_out)
        quarter_lead_times.append(second_out)
    return jnp.stack([jnp.stack(daily_lead_times), jnp.stack(quarter_lead_times)])
```

```python
import functools

import jax
import jax.numpy as jnp
import numpy as np
from jax import lax
from jax.experimental import pallas as pl
from jax.experimental.pallas import tpu as pltpu
from jax.sharding import PartitionSpec as P

WZ = 2
WH = 6
WW = 12
HALF = WH // 2
C = 192
HEADS = 6
DIM = C // HEADS
WIN = WZ * WH * WW
SPAN = 2 * WW - 1
MLP = 768
EPS = 1e-05
LOG2E = 1.4426950408889634
BF = jnp.bfloat16
F32 = jnp.float32
PACK_ROWS = 208
SLOT = 256

VMEM = pl.BlockSpec(memory_space=pltpu.VMEM)
PARAMS = pltpu.CompilerParams(vmem_limit_bytes=56 * 1024 * 1024)


def pick_rows():
    out = np.zeros((2, 2 * WIN, 1), np.int32)
    for core in range(2):
        for row in range(2 * WIN):
            w, rest = divmod(row, WIN)
            wl, zh = divmod(rest, WZ * WH)
            z, hh = divmod(zh, WH)
            half, h = divmod(hh, HALF)
            lon = (2 * core + w) * WW + wl
            out[core, row, 0] = half * 288 + (z * HALF + h) * 48 + lon
    return out


def place_rows():
    out = np.zeros((2, 288, 1), np.int32)
    for core in range(2):
        for row in range(288):
            zh, lon = divmod(row, 48)
            z, h = divmod(zh, HALF)
            w, wl = divmod(lon, WW)
            out[core, row, 0] = w * WIN + wl * WZ * WH + z * WH + HALF * core + h
    return out


def turn_columns():
    out = np.zeros((WZ * WH * SPAN, WZ * WH * SPAN), np.float32)
    for zk in range(WZ):
        for hk in range(WH):
            for j in range(SPAN):
                out[(zk * WH + hk) * SPAN + j, (SPAN - 1 - j) * WZ * WH + zk * WH + hk] = 1.0
    return out.astype(BF)


def pack_kernel(qkv, proj, expand, reduce, qkv_b, proj_b, expand_b, reduce_b, out):
    out[192:208, :] = jnp.zeros((16, 576), BF)
    out[0:192, 0:192] = expand[0]
    out[0:192, 192:336] = qkv[0]
    out[0:192, 336:384] = proj[0]
    out[0:192, 384:576] = reduce[0]
    out[192:193, 0:192] = expand_b[...]
    out[192:193, 192:336] = qkv_b[...]
    out[192:193, 336:384] = proj_b[...]
    out[192:193, 384:432] = reduce_b[...]


def one_hot(index, width):
    rows = index.shape[0]
    lanes = lax.broadcasted_iota(jnp.int32, (rows, width), 1)
    return jnp.where(lanes == index, 1.0, 0.0).astype(BF)


def norm(x, gain, shift):
    mean = jnp.sum(x, axis=-1, keepdims=True) * (1.0 / C)
    centred = x - mean
    var = jnp.sum(centred * centred, axis=-1, keepdims=True) * (1.0 / C)
    return centred * lax.rsqrt(var + EPS) * gain + shift


def dot(a, b):
    return jnp.dot(a, b, preferred_element_type=F32)


def assemble(pack, wqkv, wproj, wexp, wred, bq, bp, be, br):
    rows = slice(0, C)
    wqkv[...] = jnp.zeros_like(wqkv)
    bq[...] = jnp.zeros_like(bq)
    for j in range(4):
        wexp[:, C * j : C * (j + 1)] = pack[j, rows, 0:192]
        wproj[:, 48 * j : 48 * (j + 1)] = pack[j, rows, 336:384]
        wred[C * j : C * (j + 1), :] = pack[j, rows, 384:576]
        be[:, C * j : C * (j + 1)] = pack[j, 192:193, 0:192].astype(F32)
        bp[:, 48 * j : 48 * (j + 1)] = pack[j, 192:193, 336:384].astype(F32)
        br[:, 48 * j : 48 * (j + 1)] = pack[j, 192:193, 384:432].astype(F32)
        at = 144 * j
        while at < 144 * (j + 1):
            part, inner = divmod(at, C)
            size = min(C - inner, 144 * (j + 1) - at)
            source = slice(192 + at - 144 * j, 192 + at - 144 * j + size)
            target = slice(SLOT * part + inner, SLOT * part + inner + size)
            wqkv[:, target] = pack[j, rows, source]
            bq[:, target] = pack[j, 192:193, source].astype(F32)
            at += size


def expand_bias(table, turn, lines, bias):
    for z in range(WZ):
        for half in range(2):
            for r in range(HALF):
                zhr = z * WH + half * HALF + r
                for zk in range(WZ):
                    start = ((z * WZ + zk) * HALF + r) * WH * SPAN
                    lines[8 * zhr : 8 * zhr + HEADS, 138 * zk : 138 * (zk + 1)] = table[
                        half, :, start : start + WH * SPAN
                    ]
    whole = lines[...]
    high = whole.astype(BF)
    rest = whole - high.astype(F32)
    middle = rest.astype(BF)
    low = (rest - middle.astype(F32)).astype(BF)
    turned = (dot(high, turn[...]) + dot(middle, turn[...]) + dot(low, turn[...])) * LOG2E
    for wq in range(WW):
        start = WZ * WH * (WW - 1 - wq)
        piece = turned[:, start : start + WIN]
        for zhr in range(WZ * WH):
            row = wq * WZ * WH + zhr
            bias[:, row, :] = piece[8 * zhr : 8 * zhr + HEADS, :]


def window_block(x, gains, wqkv, wproj, wexp, wred, bq, bp, be, br, bias):
    first_gain, first_shift, second_gain, second_shift = gains
    floats = x.astype(F32)
    normed = norm(floats, first_gain, first_shift).astype(BF)
    mixed = (dot(normed, wqkv[...]) + bq[...]).astype(BF)
    q, k, v = mixed[:, 0:C], mixed[:, SLOT : SLOT + C], mixed[:, 2 * SLOT : 2 * SLOT + C]
    head_of = lax.broadcasted_iota(jnp.int32, (WIN, C), 1) // DIM
    scale = LOG2E / float(np.sqrt(DIM))
    total = None
    zero = jnp.zeros((WIN, C), BF)
    for h in range(HEADS):
        own = head_of == h
        scores = lax.dot_general(
            jnp.where(own, q, zero), k, (((1,), (1,)), ((), ())), preferred_element_type=F32
        )
        scores = scores * scale + bias[h]
        top = jnp.max(scores, axis=-1, keepdims=True)
        weights = jnp.exp2(scores - top)
        probs = (weights * (1.0 / jnp.sum(weights, axis=-1, keepdims=True))).astype(BF)
        part = dot(probs, jnp.where(own, v, zero))
        total = part if total is None else total + part
    middle = (floats + dot(total.astype(BF), wproj[...]) + bp[...]).astype(BF)
    middle_floats = middle.astype(F32)
    normed_two = norm(middle_floats, second_gain, second_shift).astype(BF)
    pre = dot(normed_two, wexp[...]) + be[...]
    hidden = (0.5 * pre * (1.0 + lax.erf(pre * float(np.sqrt(0.5))))).astype(BF)
    return (middle_floats + dot(hidden, wred[...]) + br[...]).astype(BF)


def prepare(pack, gain_refs, table, turn, lines, bias, mats):
    assemble(pack, *mats)
    lines[...] = jnp.zeros_like(lines)
    expand_bias(table, turn, lines, bias)
    return tuple(ref[...].astype(F32) for ref in gain_refs)


def first_kernel(field, index, pack, g1, s1, g2, s2, table, turn, out, lines, bias, *mats):
    @pl.when(lax.axis_index("section") == 0)
    def _():
        core = lax.rem(lax.axis_index("lat"), 2)
        gains = prepare(pack, (g1, s1, g2, s2), table, turn, lines, bias, mats)
        chosen = one_hot(index[core], 576)
        for t in range(2):
            source = jnp.concatenate([field[0, t], field[1, t]], axis=0)
            tokens = dot(chosen, source).astype(BF)
            for w in range(2):
                x = tokens[WIN * w : WIN * (w + 1)]
                out[t, WIN * w : WIN * (w + 1), :] = window_block(x, gains, *mats, bias)


def second_kernel(received, own, pack, g1, s1, g2, s2, table, turn, out, lines, bias, *mats):
    section = lax.axis_index("section")

    @pl.when(section == 0)
    def _():
        out[...] = own[...]

    @pl.when(section == 1)
    def _():
        gains = prepare(pack, (g1, s1, g2, s2), table, turn, lines, bias, mats)
        for t in range(2):
            for w in range(2):
                rows = slice(WIN * w, WIN * (w + 1))
                out[t, rows, :] = window_block(received[t, rows, :], gains, *mats, bias)


def place_kernel(windows, index, out):
    core = lax.rem(lax.axis_index("lat"), 2)
    chosen = one_hot(index[core], 576)
    for t in range(2):
        source = jnp.concatenate([windows[0, t], windows[1, t]], axis=0)
        out[t] = dot(chosen, source).astype(BF)


def call(kernel, out_shape, args, scratch=(), flops=0):
    return pl.pallas_call(
        kernel,
        out_shape=out_shape,
        in_specs=[VMEM] * len(args),
        out_specs=VMEM,
        scratch_shapes=list(scratch),
        compiler_params=PARAMS,
        cost_estimate=pl.CostEstimate(flops=flops, bytes_accessed=1 << 20, transcendentals=0),
    )(*args)


def on_device(
    initial_field,
    first_gain,
    first_shift,
    qkv_weight,
    qkv_bias,
    proj_weight,
    proj_bias,
    second_gain,
    second_shift,
    expand_weight,
    expand_bias_row,
    reduce_weight,
    reduce_bias,
    earth_bias,
):
    lat_count = lax.axis_size("lat")
    pairs = [[2 * i, 2 * i + 1] for i in range(lat_count // 2)]
    packed = call(
        pack_kernel,
        jax.ShapeDtypeStruct((PACK_ROWS, 576), BF),
        (
            qkv_weight,
            proj_weight,
            expand_weight,
            reduce_weight,
            qkv_bias,
            proj_bias,
            expand_bias_row,
            reduce_bias,
        ),
    )
    pack = lax.all_gather(packed, "tp")
    field = lax.all_gather(initial_field.reshape(2, 288, C), "lat", axis_index_groups=pairs)
    table = lax.all_gather(earth_bias.reshape(HEADS, -1), "lat", axis_index_groups=pairs)
    turn = jnp.asarray(turn_columns())
    gains = (first_gain, first_shift, second_gain, second_shift)
    scratch = [
        pltpu.VMEM((96, WZ * WH * SPAN), F32),
        pltpu.VMEM((HEADS, WIN, WIN), F32),
        pltpu.VMEM((C, 3 * SLOT), BF),
        pltpu.VMEM((C, C), BF),
        pltpu.VMEM((C, MLP), BF),
        pltpu.VMEM((MLP, C), BF),
        pltpu.VMEM((1, 3 * SLOT), F32),
        pltpu.VMEM((1, C), F32),
        pltpu.VMEM((1, MLP), F32),
        pltpu.VMEM((1, C), F32),
    ]
    shape = jax.ShapeDtypeStruct((2, 288, C), BF)
    flops = 2 * 576 * 192 * 192 * 14
    daily = call(
        first_kernel,
        shape,
        (field, jnp.asarray(pick_rows()), pack, *gains, table, turn),
        scratch,
        flops,
    )
    received = lax.ppermute(daily, "section", [(0, 1)])
    states = call(second_kernel, shape, (received, daily, pack, *gains, table, turn), scratch, flops)
    both = lax.all_gather(states, "lat", axis_index_groups=pairs)
    placed = call(place_kernel, shape, (both, jnp.asarray(place_rows())))
    return placed.reshape(1, 2, 2, 3, 48, C)


def solution(mesh):
    return jax.shard_map(
        on_device,
        mesh=mesh,
        in_specs=(
            P(None, "tp", "lat", None, None),
            P("section", None),
            P("section", None),
            P("section", None, "tp"),
            P("section", "tp"),
            P("section", None, "tp"),
            P("section", "tp"),
            P("section", None),
            P("section", None),
            P("section", None, "tp"),
            P("section", "tp"),
            P("section", "tp", None),
            P("section", "tp"),
            P("section", "tp", "lat", None, None),
        ),
        out_specs=P("section", None, "tp", "lat", None, None),
        check_vma=False,
    )
```

```python
import jax
import jax.numpy as jnp
import numpy as np
from jax import lax
from jax.experimental import pallas as pl
from jax.experimental.pallas import tpu as pltpu
from jax.sharding import PartitionSpec as P

WZ = 2
WH = 6
WW = 12
HALF = WH // 2
C = 192
HEADS = 6
DIM = C // HEADS
WIN = WZ * WH * WW
SPAN = 2 * WW - 1
KEYS = WZ * WH
LINE = KEYS * SPAN
MLP = 768
EPS = 1e-05
LOG2E = 1.4426950408889634
BF = jnp.bfloat16
F32 = jnp.float32
TOKENS = 576
SIDE = WH * SPAN

VMEM = pl.BlockSpec(memory_space=pltpu.VMEM)
PARAMS = pltpu.CompilerParams(vmem_limit_bytes=20 * 1024 * 1024)


def pick_rows():
    out = np.zeros((2, 2 * WIN, TOKENS), np.float32)
    for core in range(2):
        for row in range(2 * WIN):
            w, rest = divmod(row, WIN)
            wl, zh = divmod(rest, WZ * WH)
            z, hh = divmod(zh, WH)
            half, h = divmod(hh, HALF)
            lon = (2 * core + w) * WW + wl
            out[core, row, half * 288 + (z * HALF + h) * 48 + lon] = 1.0
    return out.astype(BF)


def split_rows():
    out = np.zeros((2 * WIN, 2 * WIN), np.float32)
    for row in range(2 * WIN):
        w, rest = divmod(row, WIN)
        wl, zh = divmod(rest, WZ * WH)
        z, hh = divmod(zh, WH)
        half, h = divmod(hh, HALF)
        out[((half * WZ + z) * HALF + h) * 24 + w * WW + wl, row] = 1.0
    return out.astype(BF)


def turn_columns():
    out = np.zeros((LINE, LINE), np.float32)
    for key in range(KEYS):
        for j in range(SPAN):
            out[key * SPAN + j, (SPAN - 1 - j) * KEYS + key] = 1.0
    return out.astype(BF)


def pack_kernel(
    qkv, proj, expand, reduce, qkv_b, proj_b, expand_b, reduce_b, field, table, weights, tokens, lines
):
    weights[288:304, :] = jnp.zeros((16, 384), BF)
    weights[0:144, 0:192] = qkv[0]
    weights[144:192, 0:192] = proj[0]
    weights[0:192, 192:384] = expand[0]
    weights[192:288, 0:192] = reduce[0, 0:96]
    weights[192:288, 192:384] = reduce[0, 96:192]
    weights[288:289, 0:144] = qkv_b[...]
    weights[288:289, 144:192] = proj_b[...]
    weights[288:289, 192:384] = expand_b[...]
    weights[289:290, 0:48] = reduce_b[...]
    tokens[0:TOKENS, 0:C] = field[...]
    lines[...] = jnp.zeros_like(lines)
    for zr in range(WZ * HALF):
        z, r = divmod(zr, HALF)
        for zk in range(WZ):
            start = ((z * WZ + zk) * HALF + r) * SIDE
            lines[zk, 8 * zr : 8 * zr + HEADS, :] = table[:, start : start + SIDE]
    for zk in range(WZ):
        whole = lines[zk]
        high = whole.astype(BF)
        rest = whole - high.astype(F32)
        middle = rest.astype(BF)
        low = (rest - middle.astype(F32)).astype(BF)
        for i, part in enumerate((high, middle, low)):
            at = TOKENS + 144 * zk + 48 * i
            tokens[at : at + 48, 0:SIDE] = part


def norm(x, gain, shift):
    mean = jnp.sum(x, axis=-1, keepdims=True) * (1.0 / C)
    centred = x - mean
    var = jnp.sum(centred * centred, axis=-1, keepdims=True) * (1.0 / C)
    return centred * lax.rsqrt(var + EPS) * gain + shift


def dot(a, b):
    return jnp.dot(a, b, preferred_element_type=F32)


def dot_t(a, b):
    return lax.dot_general(a, b, (((1,), (1,)), ((), ())), preferred_element_type=F32)


def assemble(pack, wqkv, wproj, wexp, wred, bqkv, brow):
    for j in range(4):
        wqkv[144 * j : 144 * (j + 1), :] = pack[j, 0:144, 0:192]
        wproj[48 * j : 48 * (j + 1), :] = pack[j, 144:192, 0:192]
        wexp[:, C * j : C * (j + 1)] = pack[j, 0:192, 192:384]
        wred[C * j : C * j + 96, :] = pack[j, 192:288, 0:192]
        wred[C * j + 96 : C * (j + 1), :] = pack[j, 192:288, 192:384]
        brow[0:1, C * j : C * (j + 1)] = pack[j, 288:289, 192:384].astype(F32)
        brow[1:2, 48 * j : 48 * (j + 1)] = pack[j, 288:289, 144:192].astype(F32)
        brow[2:3, 48 * j : 48 * (j + 1)] = pack[j, 289:290, 0:48].astype(F32)
        at = 144 * j
        while at < 144 * (j + 1):
            part, inner = divmod(at, C)
            size = min(C - inner, 144 * (j + 1) - at)
            source = at - 144 * j
            bqkv[part : part + 1, inner : inner + size] = pack[
                j, 288:289, source : source + size
            ].astype(F32)
            at += size


def expand_bias(field, turn, bias):
    for half in range(2):
        parts = None
        for zk in range(WZ):
            rows = slice(TOKENS + 144 * zk, TOKENS + 144 * (zk + 1))
            part = dot(field[half, rows, 0:SIDE], turn[SIDE * zk : SIDE * (zk + 1), :])
            parts = part if parts is None else parts + part
        turned = (parts[0:48] + parts[48:96] + parts[96:144]) * LOG2E
        for wq in range(WW):
            start = KEYS * (WW - 1 - wq)
            piece = turned[:, start : start + WIN]
            for zr in range(WZ * HALF):
                z, r = divmod(zr, HALF)
                row = wq * KEYS + z * WH + half * HALF + r
                bias[:, row, :] = piece[8 * zr : 8 * zr + HEADS, :]


def window_block(x, gains, wqkv, wproj, wexp, wred, bqkv, brow, bias):
    first_gain, first_shift, second_gain, second_shift = gains
    floats = x.astype(F32)
    normed = norm(floats, first_gain, first_shift).astype(BF)
    q, k, v = (
        (dot_t(normed, wqkv[C * i : C * (i + 1), :]) + bqkv[i : i + 1, :]).astype(BF)
        for i in range(3)
    )
    head_of = lax.broadcasted_iota(jnp.int32, (WIN, C), 1) // DIM
    scale = LOG2E / float(np.sqrt(DIM))
    total = None
    zero = jnp.zeros((WIN, C), BF)
    for h in range(HEADS):
        own = head_of == h
        scores = dot_t(jnp.where(own, q, zero), k) * scale + bias[h]
        top = jnp.max(scores, axis=-1, keepdims=True)
        weights = jnp.exp2(scores - top)
        probs = (weights * (1.0 / jnp.sum(weights, axis=-1, keepdims=True))).astype(BF)
        part = dot(probs, jnp.where(own, v, zero))
        total = part if total is None else total + part
    middle = (floats + dot_t(total.astype(BF), wproj[...]) + brow[1:2, 0:C]).astype(BF)
    middle_floats = middle.astype(F32)
    normed_two = norm(middle_floats, second_gain, second_shift).astype(BF)
    pre = dot(normed_two, wexp[...]) + brow[0:1, :]
    hidden = (0.5 * pre * (1.0 + lax.erf(pre * float(np.sqrt(0.5))))).astype(BF)
    return (middle_floats + dot(hidden, wred[...]) + brow[2:3, 0:C]).astype(BF)


def first_kernel(field, pick, pack, g1, s1, g2, s2, turn, out, bias, *mats):
    assemble(pack, *mats)
    expand_bias(field, turn, bias)

    @pl.when(lax.axis_index("section") == 0)
    def _():
        gains = tuple(ref[...].astype(F32) for ref in (g1, s1, g2, s2))
        chosen = pick[lax.rem(lax.axis_index("lat"), 2)]
        for t in range(2):
            rows = slice(288 * t, 288 * (t + 1))
            source = jnp.concatenate([field[0, rows, 0:C], field[1, rows, 0:C]], axis=0)
            tokens = dot(chosen, source).astype(BF)
            for w in range(2):
                x = tokens[WIN * w : WIN * (w + 1)]
                out[t, WIN * w : WIN * (w + 1), :] = window_block(x, gains, *mats, bias)


def second_kernel(received, own, split, g1, s1, g2, s2, bias, *rest):
    *mats, out, hold = rest
    section = lax.axis_index("section")

    @pl.when(section == 0)
    def _():
        hold[...] = own[...]

    @pl.when(section == 1)
    def _():
        gains = tuple(ref[...].astype(F32) for ref in (g1, s1, g2, s2))
        for t in range(2):
            for w in range(2):
                rows = slice(WIN * w, WIN * (w + 1))
                hold[t, rows, :] = window_block(received[t, rows, :], gains, *mats, bias)

    for t in range(2):
        ordered = dot(split[...], hold[t]).astype(BF)
        out[0, t] = ordered[0:WIN]
        out[1, t] = ordered[WIN : 2 * WIN]


def place_kernel(both, out, sems):
    core = lax.rem(lax.axis_index("lat"), 2)
    copies = [
        pltpu.make_async_copy(both.at[side, core], out.at[:, pl.ds(24 * side, 24), :], sems.at[side])
        for side in range(2)
    ]
    for copy in copies:
        copy.start()
    for copy in copies:
        copy.wait()


def call(kernel, out_shape, args, scratch=(), flops=0):
    many = isinstance(out_shape, tuple)
    return pl.pallas_call(
        kernel,
        out_shape=out_shape,
        in_specs=[VMEM] * len(args),
        out_specs=(VMEM,) * len(out_shape) if many else VMEM,
        scratch_shapes=list(scratch),
        compiler_params=PARAMS,
        cost_estimate=pl.CostEstimate(flops=flops, bytes_accessed=1 << 20, transcendentals=0),
    )(*args)


def on_device(
    initial_field,
    first_gain,
    first_shift,
    qkv_weight,
    qkv_bias,
    proj_weight,
    proj_bias,
    second_gain,
    second_shift,
    expand_weight,
    expand_bias_row,
    reduce_weight,
    reduce_bias,
    earth_bias,
):
    lat_count = lax.axis_size("lat")
    pairs = [[2 * i, 2 * i + 1] for i in range(lat_count // 2)]
    shape = jax.ShapeDtypeStruct
    weights, tokens = call(
        pack_kernel,
        (shape((304, 384), BF), shape((TOKENS + 288, 256), BF)),
        (
            jnp.swapaxes(qkv_weight, 1, 2),
            jnp.swapaxes(proj_weight, 1, 2),
            expand_weight,
            reduce_weight,
            qkv_bias,
            proj_bias,
            expand_bias_row,
            reduce_bias,
            initial_field.reshape(TOKENS, C),
            earth_bias.reshape(HEADS, -1),
        ),
        [pltpu.VMEM((WZ, 48, SIDE), F32)],
    )
    field = lax.all_gather(tokens, "lat", axis_index_groups=pairs)
    pack = lax.all_gather(weights, "tp")
    gains = (first_gain, first_shift, second_gain, second_shift)
    mats = (
        shape((3 * C, C), BF),
        shape((C, C), BF),
        shape((C, MLP), BF),
        shape((MLP, C), BF),
        shape((3, C), F32),
        shape((3, MLP), F32),
    )
    flops = 2 * 576 * 192 * 192 * 14
    daily, bias, *mats = call(
        first_kernel,
        (shape((2, 288, C), BF), shape((HEADS, WIN, WIN), F32), *mats),
        (field, jnp.asarray(pick_rows()), pack, *gains, jnp.asarray(turn_columns())),
        flops=flops,
    )
    received = lax.ppermute(daily, "section", [(0, 1)])
    states = call(
        second_kernel,
        shape((2, 2, WIN, C), BF),
        (received, daily, jnp.asarray(split_rows()), *gains, bias, *mats),
        [pltpu.VMEM((2, 288, C), BF)],
        flops,
    )
    both = lax.all_gather(states, "lat", axis_index_groups=pairs)
    placed = pl.pallas_call(
        place_kernel,
        out_shape=shape((12, 48, C), BF),
        in_specs=[pl.BlockSpec(memory_space=pl.ANY)],
        out_specs=pl.BlockSpec(memory_space=pl.ANY),
        scratch_shapes=[pltpu.SemaphoreType.DMA((2,))],
        compiler_params=PARAMS,
    )(both.reshape(2, 2, 12, 24, C))
    return placed.reshape(1, 2, 2, 3, 48, C)


def solution(mesh):
    return jax.shard_map(
        on_device,
        mesh=mesh,
        in_specs=(
            P(None, "tp", "lat", None, None),
            P("section", None),
            P("section", None),
            P("section", None, "tp"),
            P("section", "tp"),
            P("section", None, "tp"),
            P("section", "tp"),
            P("section", None),
            P("section", None),
            P("section", None, "tp"),
            P("section", "tp"),
            P("section", "tp", None),
            P("section", "tp"),
            P("section", "tp", "lat", None, None),
        ),
        out_specs=P("section", None, "tp", "lat", None, None),
        check_vma=False,
    )
```

```python
import jax
import jax.numpy as jnp
import numpy as np
from jax import lax
from jax.experimental import pallas as pl
from jax.experimental.pallas import tpu as pltpu
from jax.sharding import PartitionSpec as P

WZ = 2
WH = 6
WW = 12
HALF = WH // 2
C = 192
HEADS = 6
DIM = C // HEADS
WIN = WZ * WH * WW
SPAN = 2 * WW - 1
KEYS = WZ * WH
LINE = KEYS * SPAN
MLP = 768
EPS = 1e-05
LOG2E = 1.4426950408889634
BF = jnp.bfloat16
F32 = jnp.float32
TOKENS = 576
SIDE = WH * SPAN

VMEM = pl.BlockSpec(memory_space=pltpu.VMEM)
PARAMS = pltpu.CompilerParams(vmem_limit_bytes=20 * 1024 * 1024)


def pick_rows():
    out = np.zeros((2, 2 * WIN, TOKENS), np.float32)
    for core in range(2):
        for row in range(2 * WIN):
            w, rest = divmod(row, WIN)
            wl, zh = divmod(rest, WZ * WH)
            z, hh = divmod(zh, WH)
            half, h = divmod(hh, HALF)
            lon = (2 * core + w) * WW + wl
            out[core, row, half * 288 + (z * HALF + h) * 48 + lon] = 1.0
    return out.astype(BF)


def split_rows():
    out = np.zeros((2 * WIN, 2 * WIN), np.float32)
    for row in range(2 * WIN):
        w, rest = divmod(row, WIN)
        wl, zh = divmod(rest, WZ * WH)
        z, hh = divmod(zh, WH)
        half, h = divmod(hh, HALF)
        out[((half * WZ + z) * HALF + h) * 24 + w * WW + wl, row] = 1.0
    return out.astype(BF)


def turn_columns():
    out = np.zeros((LINE, LINE), np.float32)
    for key in range(KEYS):
        for j in range(SPAN):
            out[key * SPAN + j, (SPAN - 1 - j) * KEYS + key] = 1.0
    return out.astype(BF)


def load_kernel(
    qkv,
    proj,
    expand,
    reduce,
    qkv_b,
    proj_b,
    expand_b,
    reduce_b,
    field,
    table,
    pick,
    turn,
    split,
    g1,
    s1,
    g2,
    s2,
    weights,
    tokens,
    pick_out,
    turn_out,
    split_out,
    gains_out,
    qkv_v,
    proj_v,
    expand_v,
    reduce_v,
    qkv_bv,
    proj_bv,
    expand_bv,
    reduce_bv,
    field_v,
    table_v,
    gains_v,
    lines,
    sems,
):
    core = lax.rem(lax.axis_index("lat"), 2)
    moves = [(table.at[h], table_v.at[pl.ds(h, 1), :]) for h in range(HEADS)]
    moves += [
        (qkv.at[0], qkv_v),
        (proj.at[0], proj_v),
        (expand.at[0], expand_v),
        (reduce.at[0], reduce_v),
        (qkv_b, qkv_bv),
        (proj_b, proj_bv),
        (expand_b, expand_bv),
        (reduce_b, reduce_bv),
        (field, field_v),
    ]
    moves += [(ref, gains_v.at[i]) for i, ref in enumerate((g1, s1, g2, s2))]
    moves += [(pick.at[core], pick_out), (turn, turn_out), (split, split_out)]
    copies = [pltpu.make_async_copy(a, b, sems.at[i]) for i, (a, b) in enumerate(moves)]
    for copy in copies:
        copy.start()
    weights[288:304, :] = jnp.zeros((16, 384), BF)
    lines[...] = jnp.zeros_like(lines)
    for copy in copies[:HEADS]:
        copy.wait()
    for zr in range(WZ * HALF):
        z, r = divmod(zr, HALF)
        for zk in range(WZ):
            start = ((z * WZ + zk) * HALF + r) * SIDE
            lines[zk, 8 * zr : 8 * zr + HEADS, :] = table_v[0:HEADS, start : start + SIDE]
    for zk in range(WZ):
        whole = lines[zk]
        high = whole.astype(BF)
        rest = whole - high.astype(F32)
        middle = rest.astype(BF)
        low = (rest - middle.astype(F32)).astype(BF)
        for i, part in enumerate((high, middle, low)):
            at = TOKENS + 144 * zk + 48 * i
            tokens[at : at + 48, 0:SIDE] = part
    for copy in copies[HEADS:]:
        copy.wait()
    weights[0:144, 0:192] = qkv_v[...]
    weights[144:192, 0:192] = proj_v[...]
    weights[0:192, 192:384] = expand_v[...]
    weights[192:288, 0:192] = reduce_v[0:96, :]
    weights[192:288, 192:384] = reduce_v[96:192, :]
    weights[288:289, 0:144] = qkv_bv[...]
    weights[288:289, 144:192] = proj_bv[...]
    weights[288:289, 192:384] = expand_bv[...]
    weights[289:290, 0:48] = reduce_bv[...]
    tokens[0:TOKENS, 0:C] = field_v[...]
    for i in range(4):
        gains_out[i : i + 1, :] = gains_v[i].astype(F32)


def norm(x, gain, shift):
    mean = jnp.sum(x, axis=-1, keepdims=True) * (1.0 / C)
    centred = x - mean
    var = jnp.sum(centred * centred, axis=-1, keepdims=True) * (1.0 / C)
    return centred * lax.rsqrt(var + EPS) * gain + shift


def dot(a, b):
    return jnp.dot(a, b, preferred_element_type=F32)


def dot_t(a, b):
    return lax.dot_general(a, b, (((1,), (1,)), ((), ())), preferred_element_type=F32)


def assemble(pack, wqkv, wproj, wexp, wred, bqkv, brow):
    for j in range(4):
        wqkv[144 * j : 144 * (j + 1), :] = pack[j, 0:144, 0:192]
        wproj[48 * j : 48 * (j + 1), :] = pack[j, 144:192, 0:192]
        wexp[:, C * j : C * (j + 1)] = pack[j, 0:192, 192:384]
        wred[C * j : C * j + 96, :] = pack[j, 192:288, 0:192]
        wred[C * j + 96 : C * (j + 1), :] = pack[j, 192:288, 192:384]
        brow[0:1, C * j : C * (j + 1)] = pack[j, 288:289, 192:384].astype(F32)
        brow[1:2, 48 * j : 48 * (j + 1)] = pack[j, 288:289, 144:192].astype(F32)
        brow[2:3, 48 * j : 48 * (j + 1)] = pack[j, 289:290, 0:48].astype(F32)
        at = 144 * j
        while at < 144 * (j + 1):
            part, inner = divmod(at, C)
            size = min(C - inner, 144 * (j + 1) - at)
            source = at - 144 * j
            bqkv[part : part + 1, inner : inner + size] = pack[
                j, 288:289, source : source + size
            ].astype(F32)
            at += size


def expand_bias(field, turn, bias):
    for half in range(2):
        parts = None
        for zk in range(WZ):
            rows = slice(TOKENS + 144 * zk, TOKENS + 144 * (zk + 1))
            part = dot(field[half, rows, 0:SIDE], turn[SIDE * zk : SIDE * (zk + 1), :])
            parts = part if parts is None else parts + part
        turned = (parts[0:48] + parts[48:96] + parts[96:144]) * LOG2E
        for wq in range(WW):
            start = KEYS * (WW - 1 - wq)
            piece = turned[:, start : start + WIN]
            for zr in range(WZ * HALF):
                z, r = divmod(zr, HALF)
                row = wq * KEYS + z * WH + half * HALF + r
                bias[:, row, :] = piece[8 * zr : 8 * zr + HEADS, :]


def attend(q, k, v, bias):
    head_of = lax.broadcasted_iota(jnp.int32, (WIN, C), 1) // DIM
    scale = LOG2E / float(np.sqrt(DIM))
    zero = jnp.zeros((WIN, C), BF)
    stacked = jnp.concatenate([jnp.where(head_of == h, q, zero) for h in range(HEADS)], axis=0)
    scores = dot_t(stacked, k)
    probs, inverse = [], []
    for h in range(HEADS):
        own = scores[WIN * h : WIN * (h + 1)] * scale + bias[h]
        weights = jnp.exp2(own - jnp.max(own, axis=-1, keepdims=True))
        inverse.append(1.0 / jnp.sum(weights, axis=-1, keepdims=True))
        probs.append(weights.astype(BF))
    values = dot(jnp.concatenate(probs, axis=0), v)
    total = values[0:WIN] * inverse[0]
    for h in range(1, HEADS):
        part = values[WIN * h : WIN * (h + 1)] * inverse[h]
        total = jnp.where(head_of == h, part, total)
    return total.astype(BF)


def block(x, gains, wqkv, wproj, wexp, wred, bqkv, brow, bias, queries, keys, values, attended):
    floats = x.astype(F32)
    normed = norm(floats, gains[0:1, :], gains[1:2, :]).astype(BF)
    for i, ref in enumerate((queries, keys, values)):
        ref[...] = (dot_t(normed, wqkv[C * i : C * (i + 1), :]) + bqkv[i : i + 1, :]).astype(BF)
    for w in range(TOKENS // WIN):
        rows = slice(WIN * w, WIN * (w + 1))
        attended[rows, :] = attend(queries[rows, :], keys[rows, :], values[rows, :], bias)
    middle = (floats + dot_t(attended[...], wproj[...]) + brow[1:2, 0:C]).astype(BF)
    middle_floats = middle.astype(F32)
    normed_two = norm(middle_floats, gains[2:3, :], gains[3:4, :]).astype(BF)
    pre = dot(normed_two, wexp[...]) + brow[0:1, :]
    hidden = (0.5 * pre * (1.0 + lax.erf(pre * float(np.sqrt(0.5))))).astype(BF)
    return (middle_floats + dot(hidden, wred[...]) + brow[2:3, 0:C]).astype(BF)


def first_kernel(field, pick, pack, gains, turn, out, bias, *rest):
    *mats, tokens, queries, keys, values, attended = rest
    section = lax.axis_index("section")
    assemble(pack, *mats)
    expand_bias(field, turn, bias)

    @pl.when(section == 0)
    def _():
        for t in range(2):
            rows = slice(288 * t, 288 * (t + 1))
            source = jnp.concatenate([field[0, rows, 0:C], field[1, rows, 0:C]], axis=0)
            tokens[rows, :] = dot(pick[...], source).astype(BF)
        result = block(tokens[...], gains, *mats, bias, queries, keys, values, attended)
        out[:, 0:C] = result[0:288]
        out[:, C : 2 * C] = result[288:576]


def second_kernel(received, own, split, gains, bias, *rest):
    *mats, out, hold, tokens, queries, keys, values, attended = rest
    section = lax.axis_index("section")

    @pl.when(section == 0)
    def _():
        hold[0:288, :] = own[:, 0:C]
        hold[288:576, :] = own[:, C : 2 * C]

    @pl.when(section == 1)
    def _():
        tokens[0:288, :] = received[:, 0:C]
        tokens[288:576, :] = received[:, C : 2 * C]
        hold[...] = block(tokens[...], gains, *mats, bias, queries, keys, values, attended)

    for t in range(2):
        ordered = dot(split[...], hold[288 * t : 288 * (t + 1), :]).astype(BF)
        out[0, t] = ordered[0:WIN]
        out[1, t] = ordered[WIN : 2 * WIN]


def place_kernel(both, out, sems):
    core = lax.rem(lax.axis_index("lat"), 2)
    copies = [
        pltpu.make_async_copy(both.at[side, core], out.at[:, pl.ds(24 * side, 24), :], sems.at[side])
        for side in range(2)
    ]
    for copy in copies:
        copy.start()
    for copy in copies:
        copy.wait()


def call(kernel, out_shape, args, scratch=(), flops=0):
    many = isinstance(out_shape, tuple)
    return pl.pallas_call(
        kernel,
        out_shape=out_shape,
        in_specs=[VMEM] * len(args),
        out_specs=(VMEM,) * len(out_shape) if many else VMEM,
        scratch_shapes=list(scratch),
        compiler_params=PARAMS,
        cost_estimate=pl.CostEstimate(flops=flops, bytes_accessed=1 << 20, transcendentals=0),
    )(*args)


def on_device(
    initial_field,
    first_gain,
    first_shift,
    qkv_weight,
    qkv_bias,
    proj_weight,
    proj_bias,
    second_gain,
    second_shift,
    expand_weight,
    expand_bias_row,
    reduce_weight,
    reduce_bias,
    earth_bias,
):
    lat_count = lax.axis_size("lat")
    pairs = [[2 * i, 2 * i + 1] for i in range(lat_count // 2)]
    shape = jax.ShapeDtypeStruct
    hbm = pl.BlockSpec(memory_space=pltpu.HBM)
    operands = (
        jnp.swapaxes(qkv_weight, 1, 2),
        jnp.swapaxes(proj_weight, 1, 2),
        expand_weight,
        reduce_weight,
        qkv_bias,
        proj_bias,
        expand_bias_row,
        reduce_bias,
        initial_field.reshape(TOKENS, C),
        earth_bias.reshape(HEADS, 1, -1),
        jnp.asarray(pick_rows()),
        jnp.asarray(turn_columns()),
        jnp.asarray(split_rows()),
        first_gain,
        first_shift,
        second_gain,
        second_shift,
    )
    weights, tokens, pick, turn, split, gains = pl.pallas_call(
        load_kernel,
        out_shape=(
            shape((304, 384), BF),
            shape((TOKENS + 288, 256), BF),
            shape((288, TOKENS), BF),
            shape((LINE, LINE), BF),
            shape((288, 288), BF),
            shape((4, C), F32),
        ),
        in_specs=[hbm] * len(operands),
        out_specs=(VMEM,) * 6,
        scratch_shapes=[
            pltpu.VMEM((144, C), BF),
            pltpu.VMEM((48, C), BF),
            pltpu.VMEM((C, C), BF),
            pltpu.VMEM((C, C), BF),
            pltpu.VMEM((1, 144), BF),
            pltpu.VMEM((1, 48), BF),
            pltpu.VMEM((1, C), BF),
            pltpu.VMEM((1, 48), BF),
            pltpu.VMEM((TOKENS, C), BF),
            pltpu.VMEM((8, 1656), F32),
            pltpu.VMEM((4, 1, C), BF),
            pltpu.VMEM((WZ, 48, SIDE), F32),
            pltpu.SemaphoreType.DMA((22,)),
        ],
        compiler_params=PARAMS,
    )(*(pltpu.with_memory_space_constraint(x, pltpu.HBM) for x in operands))
    field = lax.all_gather(tokens, "lat", axis_index_groups=pairs)
    pack = lax.all_gather(weights, "tp")
    mats = (
        shape((3 * C, C), BF),
        shape((C, C), BF),
        shape((C, MLP), BF),
        shape((MLP, C), BF),
        shape((3, C), F32),
        shape((3, MLP), F32),
    )
    stages = [pltpu.VMEM((TOKENS, C), BF)] * 5
    flops = 2 * 576 * 192 * 192 * 14
    daily, bias, *mats = call(
        first_kernel,
        (shape((288, 2 * C), BF), shape((HEADS, WIN, WIN), F32), *mats),
        (field, pick, pack, gains, turn),
        stages,
        flops,
    )
    received = lax.ppermute(daily, "section", [(0, 1)])
    states = call(
        second_kernel,
        shape((2, 2, WIN, C), BF),
        (received, daily, split, gains, bias, *mats),
        [pltpu.VMEM((TOKENS, C), BF)] + stages,
        flops,
    )
    both = lax.all_gather(states, "lat", axis_index_groups=pairs)
    placed = pl.pallas_call(
        place_kernel,
        out_shape=shape((12, 48, C), BF),
        in_specs=[pl.BlockSpec(memory_space=pl.ANY)],
        out_specs=pl.BlockSpec(memory_space=pl.ANY),
        scratch_shapes=[pltpu.SemaphoreType.DMA((2,))],
        compiler_params=PARAMS,
    )(both.reshape(2, 2, 12, 24, C))
    return placed.reshape(1, 2, 2, 3, 48, C)


def solution(mesh):
    return jax.shard_map(
        on_device,
        mesh=mesh,
        in_specs=(
            P(None, "tp", "lat", None, None),
            P("section", None),
            P("section", None),
            P("section", None, "tp"),
            P("section", "tp"),
            P("section", None, "tp"),
            P("section", "tp"),
            P("section", None),
            P("section", None),
            P("section", None, "tp"),
            P("section", "tp"),
            P("section", "tp", None),
            P("section", "tp"),
            P("section", "tp", "lat", None, None),
        ),
        out_specs=P("section", None, "tp", "lat", None, None),
        check_vma=False,
    )
```

```python
import jax
import jax.numpy as jnp
import numpy as np
from jax import lax
from jax.experimental import pallas as pl
from jax.experimental.pallas import tpu as pltpu
from jax.sharding import PartitionSpec as P

WZ = 2
WH = 6
WW = 12
HALF = WH // 2
C = 192
HEADS = 6
DIM = C // HEADS
WIN = WZ * WH * WW
SPAN = 2 * WW - 1
KEYS = WZ * WH
LINE = KEYS * SPAN
MLP = 768
EPS = 1e-05
LOG2E = 1.4426950408889634
BF = jnp.bfloat16
F32 = jnp.float32
TOKENS = 576
SIDE = WH * SPAN

VMEM = pl.BlockSpec(memory_space=pltpu.VMEM)
PARAMS = pltpu.CompilerParams(vmem_limit_bytes=20 * 1024 * 1024)


def places(core):
    row = 0
    for w in range(2):
        for wl in range(WW):
            for z in range(WZ):
                for other in range(2):
                    for h in range(HALF):
                        yield row, other, z, h, w * WW + wl
                        row += 1


def pick_rows():
    out = np.zeros((2, 2 * WIN, TOKENS), np.float32)
    for core in range(2):
        for row, other, z, h, lon in places(core):
            out[core, row, other * 288 + (z * HALF + h) * 48 + 24 * core + lon] = 1.0
    return out.astype(BF)


def split_rows():
    out = np.zeros((2, 2 * WIN, 2 * WIN), np.float32)
    for core in range(2):
        for row, other, z, h, lon in places(core):
            out[core, (((core ^ other) * WZ + z) * HALF + h) * 24 + lon, row] = 1.0
    return out.astype(BF)


def turn_columns():
    out = np.zeros((2, LINE, LINE), np.float32)
    for core in range(2):
        for zk in range(WZ):
            for hk in range(WH):
                key = zk * WH + HALF * (core ^ (hk // HALF)) + hk % HALF
                for j in range(SPAN):
                    out[core, (zk * WH + hk) * SPAN + j, (SPAN - 1 - j) * KEYS + key] = 1.0
    return out.astype(BF)


def load_kernel(
    qkv,
    proj,
    expand,
    reduce,
    qkv_b,
    proj_b,
    expand_b,
    reduce_b,
    field,
    table,
    pick,
    turn,
    split,
    g1,
    s1,
    g2,
    s2,
    weights,
    tokens,
    pick_out,
    turn_out,
    split_out,
    gains_out,
    qkv_v,
    proj_v,
    expand_v,
    reduce_v,
    qkv_bv,
    proj_bv,
    expand_bv,
    reduce_bv,
    field_v,
    table_v,
    gains_v,
    lines,
    sems,
):
    core = lax.rem(lax.axis_index("lat"), 2)
    moves = [(table.at[h], table_v.at[pl.ds(h, 1), :]) for h in range(HEADS)]
    moves += [
        (qkv.at[0], qkv_v),
        (proj.at[0], proj_v),
        (expand.at[0], expand_v),
        (reduce.at[0], reduce_v),
        (qkv_b, qkv_bv),
        (proj_b, proj_bv),
        (expand_b, expand_bv),
        (reduce_b, reduce_bv),
        (field, field_v),
    ]
    moves += [(ref, gains_v.at[i]) for i, ref in enumerate((g1, s1, g2, s2))]
    moves += [(pick.at[core], pick_out), (turn.at[core], turn_out), (split.at[core], split_out)]
    copies = [pltpu.make_async_copy(a, b, sems.at[i]) for i, (a, b) in enumerate(moves)]
    for copy in copies:
        copy.start()
    weights[288:304, :] = jnp.zeros((16, 384), BF)
    lines[...] = jnp.zeros_like(lines)
    for copy in copies[:HEADS]:
        copy.wait()
    for zr in range(WZ * HALF):
        z, r = divmod(zr, HALF)
        for zk in range(WZ):
            start = ((z * WZ + zk) * HALF + r) * SIDE
            lines[zk, 8 * zr : 8 * zr + HEADS, :] = table_v[0:HEADS, start : start + SIDE]
    for zk in range(WZ):
        whole = lines[zk]
        high = whole.astype(BF)
        rest = whole - high.astype(F32)
        middle = rest.astype(BF)
        low = (rest - middle.astype(F32)).astype(BF)
        for i, part in enumerate((high, middle, low)):
            at = TOKENS + 144 * zk + 48 * i
            tokens[at : at + 48, 0:SIDE] = part
    for copy in copies[HEADS:]:
        copy.wait()
    weights[0:144, 0:192] = qkv_v[...]
    weights[144:192, 0:192] = proj_v[...]
    weights[0:192, 192:384] = expand_v[...]
    weights[192:288, 0:192] = reduce_v[0:96, :]
    weights[192:288, 192:384] = reduce_v[96:192, :]
    weights[288:289, 0:144] = qkv_bv[...]
    weights[288:289, 144:192] = proj_bv[...]
    weights[288:289, 192:384] = expand_bv[...]
    weights[289:290, 0:48] = reduce_bv[...]
    tokens[0:TOKENS, 0:C] = field_v[...]
    for i in range(4):
        gains_out[i : i + 1, :] = gains_v[i].astype(F32)


def norm(x, gain, shift):
    mean = jnp.sum(x, axis=-1, keepdims=True) * (1.0 / C)
    centred = x - mean
    var = jnp.sum(centred * centred, axis=-1, keepdims=True) * (1.0 / C)
    return centred * lax.rsqrt(var + EPS) * gain + shift


def dot(a, b):
    return jnp.dot(a, b, preferred_element_type=F32)


def dot_t(a, b):
    return lax.dot_general(a, b, (((1,), (1,)), ((), ())), preferred_element_type=F32)


def assemble(pack, wqkv, wproj, wexp, wred, bqkv, brow):
    for j in range(4):
        wqkv[144 * j : 144 * (j + 1), :] = pack[j, 0:144, 0:192]
        wproj[48 * j : 48 * (j + 1), :] = pack[j, 144:192, 0:192]
        wexp[:, C * j : C * (j + 1)] = pack[j, 0:192, 192:384]
        wred[C * j : C * j + 96, :] = pack[j, 192:288, 0:192]
        wred[C * j + 96 : C * (j + 1), :] = pack[j, 192:288, 192:384]
        brow[0:1, C * j : C * (j + 1)] = pack[j, 288:289, 192:384].astype(F32)
        brow[1:2, 48 * j : 48 * (j + 1)] = pack[j, 288:289, 144:192].astype(F32)
        brow[2:3, 48 * j : 48 * (j + 1)] = pack[j, 289:290, 0:48].astype(F32)
        at = 144 * j
        while at < 144 * (j + 1):
            part, inner = divmod(at, C)
            size = min(C - inner, 144 * (j + 1) - at)
            source = at - 144 * j
            bqkv[part : part + 1, inner : inner + size] = pack[
                j, 288:289, source : source + size
            ].astype(F32)
            at += size


def expand_bias(fields, turn, bias):
    for half, field in enumerate(fields):
        parts = None
        for zk in range(WZ):
            rows = slice(TOKENS + 144 * zk, TOKENS + 144 * (zk + 1))
            part = dot(field[rows, 0:SIDE], turn[SIDE * zk : SIDE * (zk + 1), :])
            parts = part if parts is None else parts + part
        turned = (parts[0:48] + parts[48:96] + parts[96:144]) * LOG2E
        for wq in range(WW):
            start = KEYS * (WW - 1 - wq)
            piece = turned[:, start : start + WIN]
            for zr in range(WZ * HALF):
                z, r = divmod(zr, HALF)
                row = wq * KEYS + z * WH + half * HALF + r
                bias[:, row, :] = piece[8 * zr : 8 * zr + HEADS, :]


def attend(q, k, v, bias):
    head_of = lax.broadcasted_iota(jnp.int32, (WIN, C), 1) // DIM
    scale = LOG2E / float(np.sqrt(DIM))
    zero = jnp.zeros((WIN, C), BF)
    stacked = jnp.concatenate([jnp.where(head_of == h, q, zero) for h in range(HEADS)], axis=0)
    scores = dot_t(stacked, k)
    probs, inverse = [], []
    for h in range(HEADS):
        own = scores[WIN * h : WIN * (h + 1)] * scale + bias[h]
        weights = jnp.exp2(own - jnp.max(own, axis=-1, keepdims=True))
        inverse.append(1.0 / jnp.sum(weights, axis=-1, keepdims=True))
        probs.append(weights.astype(BF))
    values = dot(jnp.concatenate(probs, axis=0), v)
    total = values[0:WIN] * inverse[0]
    for h in range(1, HEADS):
        part = values[WIN * h : WIN * (h + 1)] * inverse[h]
        total = jnp.where(head_of == h, part, total)
    return total.astype(BF)


def block(x, gains, wqkv, wproj, wexp, wred, bqkv, brow, bias):
    floats = x.astype(F32)
    normed = norm(floats, gains[0:1, :], gains[1:2, :]).astype(BF)
    q, k, v = (
        (dot_t(normed, wqkv[C * i : C * (i + 1), :]) + bqkv[i : i + 1, :]).astype(BF)
        for i in range(3)
    )
    windows = (slice(WIN * w, WIN * (w + 1)) for w in range(2))
    attended = jnp.concatenate([attend(q[rows], k[rows], v[rows], bias) for rows in windows], axis=0)
    middle = (floats + dot_t(attended, wproj[...]) + brow[1:2, 0:C]).astype(BF)
    middle_floats = middle.astype(F32)
    normed_two = norm(middle_floats, gains[2:3, :], gains[3:4, :]).astype(BF)
    total = middle_floats + brow[2:3, 0:C]
    for at in range(0, MLP, 256):
        pre = dot(normed_two, wexp[:, at : at + 256]) + brow[0:1, at : at + 256]
        hidden = (0.5 * pre * (1.0 + lax.erf(pre * float(np.sqrt(0.5))))).astype(BF)
        total = total + dot(hidden, wred[at : at + 256, :])
    return total.astype(BF)


def daily_block(t, fields, pick, out, *rest):
    rows = slice(288 * t, 288 * (t + 1))
    source = jnp.concatenate([field[rows, 0:C] for field in fields], axis=0)
    result = block(dot(pick[...], source).astype(BF), *rest)
    out[:, 0:C] = result[0:WIN]
    out[:, C : 2 * C] = result[WIN : 2 * WIN]


def prepare_kernel(own, other, pick, pack, gains, turn, out, bias, *mats):
    assemble(pack, *mats)
    expand_bias((own, other), turn, bias)

    @pl.when(lax.axis_index("section") == 0)
    def _():
        daily_block(0, (own, other), pick, out, gains, *mats, bias)


def daily_kernel(own, other, pick, gains, bias, *rest):
    *mats, out = rest

    @pl.when(lax.axis_index("section") == 0)
    def _():
        daily_block(1, (own, other), pick, out, gains, *mats, bias)


def chained_block(received, own, split, gains, bias, mats, hold):
    section = lax.axis_index("section")

    @pl.when(section == 0)
    def _():
        hold[0:WIN, :] = own[:, 0:C]
        hold[WIN : 2 * WIN, :] = own[:, C : 2 * C]

    @pl.when(section == 1)
    def _():
        hold[0:WIN, :] = received[:, 0:C]
        hold[WIN : 2 * WIN, :] = received[:, C : 2 * C]
        hold[...] = block(hold[...], gains, *mats, bias)

    return dot(split[...], hold[...]).astype(BF)


def chained_kernel(received, own, split, gains, bias, *rest):
    *mats, out, hold = rest
    ordered = chained_block(received, own, split, gains, bias, mats, hold)
    out[0] = ordered[0:WIN]
    out[1] = ordered[WIN : 2 * WIN]


def last_kernel(earlier, received, own, split, gains, bias, *rest):
    *mats, out, hold = rest
    out[0, 0] = earlier[0]
    out[1, 0] = earlier[1]
    ordered = chained_block(received, own, split, gains, bias, mats, hold)
    out[0, 1] = ordered[0:WIN]
    out[1, 1] = ordered[WIN : 2 * WIN]


def place_kernel(both, out, sems):
    core = lax.rem(lax.axis_index("lat"), 2)
    copies = [
        pltpu.make_async_copy(both.at[side, core], out.at[:, pl.ds(24 * side, 24), :], sems.at[side])
        for side in range(2)
    ]
    for copy in copies:
        copy.start()
    for copy in copies:
        copy.wait()


def call(kernel, out_shape, args, scratch=(), flops=0):
    many = isinstance(out_shape, tuple)
    return pl.pallas_call(
        kernel,
        out_shape=out_shape,
        in_specs=[VMEM] * len(args),
        out_specs=(VMEM,) * len(out_shape) if many else VMEM,
        scratch_shapes=list(scratch),
        compiler_params=PARAMS,
        cost_estimate=pl.CostEstimate(flops=flops, bytes_accessed=1 << 20, transcendentals=0),
    )(*args)


def on_device(
    initial_field,
    first_gain,
    first_shift,
    qkv_weight,
    qkv_bias,
    proj_weight,
    proj_bias,
    second_gain,
    second_shift,
    expand_weight,
    expand_bias_row,
    reduce_weight,
    reduce_bias,
    earth_bias,
):
    lat_count = lax.axis_size("lat")
    pairs = [[2 * i, 2 * i + 1] for i in range(lat_count // 2)]
    shape = jax.ShapeDtypeStruct
    hbm = pl.BlockSpec(memory_space=pltpu.HBM)
    operands = (
        jnp.swapaxes(qkv_weight, 1, 2),
        jnp.swapaxes(proj_weight, 1, 2),
        expand_weight,
        reduce_weight,
        qkv_bias,
        proj_bias,
        expand_bias_row,
        reduce_bias,
        initial_field.reshape(TOKENS, C),
        earth_bias.reshape(HEADS, 1, -1),
        jnp.asarray(pick_rows()),
        jnp.asarray(turn_columns()),
        jnp.asarray(split_rows()),
        first_gain,
        first_shift,
        second_gain,
        second_shift,
    )
    weights, tokens, pick, turn, split, gains = pl.pallas_call(
        load_kernel,
        out_shape=(
            shape((304, 384), BF),
            shape((TOKENS + 288, 256), BF),
            shape((288, TOKENS), BF),
            shape((LINE, LINE), BF),
            shape((288, 288), BF),
            shape((4, C), F32),
        ),
        in_specs=[hbm] * len(operands),
        out_specs=(VMEM,) * 6,
        scratch_shapes=[
            pltpu.VMEM((144, C), BF),
            pltpu.VMEM((48, C), BF),
            pltpu.VMEM((C, C), BF),
            pltpu.VMEM((C, C), BF),
            pltpu.VMEM((1, 144), BF),
            pltpu.VMEM((1, 48), BF),
            pltpu.VMEM((1, C), BF),
            pltpu.VMEM((1, 48), BF),
            pltpu.VMEM((TOKENS, C), BF),
            pltpu.VMEM((8, 1656), F32),
            pltpu.VMEM((4, 1, C), BF),
            pltpu.VMEM((WZ, 48, SIDE), F32),
            pltpu.SemaphoreType.DMA((22,)),
        ],
        compiler_params=PARAMS,
    )(*(pltpu.with_memory_space_constraint(x, pltpu.HBM) for x in operands))
    swap = [(i, i ^ 1) for i in range(lat_count)]
    other = lax.ppermute(tokens, "lat", swap)
    pack = lax.all_gather(weights, "tp")
    mats = (
        shape((3 * C, C), BF),
        shape((C, C), BF),
        shape((C, MLP), BF),
        shape((MLP, C), BF),
        shape((3, C), F32),
        shape((3, MLP), F32),
    )
    flops = 2 * 288 * 192 * 192 * 14
    dense = shape((WIN, 2 * C), BF)
    ahead = [(0, 1)]
    daily_0, bias, *mats = call(
        prepare_kernel,
        (dense, shape((HEADS, WIN, WIN), F32), *mats),
        (tokens, other, pick, pack, gains, turn),
        flops=flops,
    )
    received_0 = lax.ppermute(daily_0, "section", ahead)
    daily_1 = call(
        daily_kernel, dense, (tokens, other, pick, gains, bias, *mats), flops=flops
    )
    received_1 = lax.ppermute(daily_1, "section", ahead)
    hold = [pltpu.VMEM((2 * WIN, C), BF)]
    earlier = call(
        chained_kernel,
        shape((2, WIN, C), BF),
        (received_0, daily_0, split, gains, bias, *mats),
        hold,
        flops,
    )
    states = call(
        last_kernel,
        shape((2, 2, WIN, C), BF),
        (earlier, received_1, daily_1, split, gains, bias, *mats),
        hold,
        flops,
    )
    both = lax.all_gather(states, "lat", axis_index_groups=pairs)
    placed = pl.pallas_call(
        place_kernel,
        out_shape=shape((12, 48, C), BF),
        in_specs=[pl.BlockSpec(memory_space=pl.ANY)],
        out_specs=pl.BlockSpec(memory_space=pl.ANY),
        scratch_shapes=[pltpu.SemaphoreType.DMA((2,))],
        compiler_params=PARAMS,
    )(both.reshape(2, 2, 12, 24, C))
    return placed.reshape(1, 2, 2, 3, 48, C)


def solution(mesh):
    return jax.shard_map(
        on_device,
        mesh=mesh,
        in_specs=(
            P(None, "tp", "lat", None, None),
            P("section", None),
            P("section", None),
            P("section", None, "tp"),
            P("section", "tp"),
            P("section", None, "tp"),
            P("section", "tp"),
            P("section", None),
            P("section", None),
            P("section", None, "tp"),
            P("section", "tp"),
            P("section", "tp", None),
            P("section", "tp"),
            P("section", "tp", "lat", None, None),
        ),
        out_specs=P("section", None, "tp", "lat", None, None),
        check_vma=False,
    )
```

```python
import jax
import jax.numpy as jnp
import numpy as np
from jax import lax
from jax.experimental import pallas as pl
from jax.experimental.pallas import tpu as pltpu
from jax.sharding import PartitionSpec as P

WZ = 2
WH = 6
WW = 12
HALF = WH // 2
C = 192
HEADS = 6
DIM = C // HEADS
WIN = WZ * WH * WW
SPAN = 2 * WW - 1
KEYS = WZ * WH
LINE = KEYS * SPAN
MLP = 768
EPS = 1e-05
LOG2E = 1.4426950408889634
BF = jnp.bfloat16
F32 = jnp.float32
SIDE = WH * SPAN

VMEM = pl.BlockSpec(memory_space=pltpu.VMEM)
PARAMS = pltpu.CompilerParams(vmem_limit_bytes=20 * 1024 * 1024)


def places():
    row = 0
    for w in range(2):
        for wl in range(WW):
            for other in range(2):
                for z in range(WZ):
                    for h in range(HALF):
                        yield row, other, z, h, w * WW + wl
                        row += 1


def pick_rows():
    out = np.zeros((2 * WIN, 2 * WIN), np.float32)
    for row, other, z, h, lon in places():
        out[row, ((other * WZ + z) * HALF + h) * 24 + lon] = 1.0
    return out.astype(BF)


def turn_columns():
    out = np.zeros((2, LINE, LINE), np.float32)
    for core in range(2):
        for zk in range(WZ):
            for hk in range(WH):
                key = ((core ^ (hk // HALF)) * WZ + zk) * HALF + hk % HALF
                for j in range(SPAN):
                    out[core, (zk * WH + hk) * SPAN + j, (SPAN - 1 - j) * KEYS + key] = 1.0
    return out.astype(BF)


def load_kernel(
    qkv,
    proj,
    expand,
    reduce,
    qkv_b,
    proj_b,
    expand_b,
    reduce_b,
    field,
    table,
    g1,
    s1,
    g2,
    s2,
    weights,
    kept,
    sent,
    gains_out,
    qkv_v,
    proj_v,
    expand_v,
    reduce_v,
    qkv_bv,
    proj_bv,
    expand_bv,
    reduce_bv,
    kept_v,
    sent_v,
    table_v,
    gains_v,
    lines,
    sems,
):
    core = lax.rem(lax.axis_index("lat"), 2)
    moves = [(table.at[h], table_v.at[pl.ds(h, 1), :]) for h in range(HEADS)]
    moves += [
        (qkv.at[0], qkv_v),
        (proj.at[0], proj_v),
        (expand.at[0], expand_v),
        (reduce.at[0], reduce_v),
        (qkv_b, qkv_bv),
        (proj_b, proj_bv),
        (expand_b, expand_bv),
        (reduce_b, reduce_bv),
        (field.at[:, pl.ds(pl.multiple_of(24 * core, 8), 24), :], kept_v),
        (field.at[:, pl.ds(pl.multiple_of(24 - 24 * core, 8), 24), :], sent_v),
    ]
    moves += [(ref, gains_v.at[i]) for i, ref in enumerate((g1, s1, g2, s2))]
    copies = [pltpu.make_async_copy(a, b, sems.at[i]) for i, (a, b) in enumerate(moves)]
    for copy in copies:
        copy.start()
    weights[288:304, :] = jnp.zeros((16, 384), BF)
    lines[...] = jnp.zeros_like(lines)
    blank = jnp.zeros((HEADS, 256 - SIDE), F32)
    for copy in copies[:HEADS]:
        copy.wait()
    for zr in range(WZ * HALF):
        z, r = divmod(zr, HALF)
        for zk in range(WZ):
            start = ((z * WZ + zk) * HALF + r) * SIDE
            target = pl.ds(zr, HEADS, stride=8)
            lines[2 * zk, target, :] = table_v[0:HEADS, start : start + 128]
            tail = table_v[0:HEADS, start + 128 : start + SIDE]
            lines[2 * zk + 1, target, :] = jnp.concatenate([tail, blank], axis=1)
    for zk in range(WZ):
        whole = jnp.concatenate([lines[2 * zk], lines[2 * zk + 1]], axis=1)
        high = whole.astype(BF)
        rest = whole - high.astype(F32)
        middle = rest.astype(BF)
        low = (rest - middle.astype(F32)).astype(BF)
        for i, part in enumerate((high, middle, low)):
            rows = slice(288 + 144 * zk + 48 * i, 288 + 144 * zk + 48 * (i + 1))
            kept[rows, :] = part
            sent[rows, :] = part
    for copy in copies[HEADS:]:
        copy.wait()
    weights[0:144, 0:192] = qkv_v[...]
    weights[144:192, 0:192] = proj_v[...]
    weights[0:192, 192:384] = expand_v[...]
    weights[192:288, 0:192] = reduce_v[0:96, :]
    weights[192:288, 192:384] = reduce_v[96:192, :]
    weights[288:289, 0:144] = qkv_bv[...]
    weights[288:289, 144:192] = proj_bv[...]
    weights[288:289, 192:384] = expand_bv[...]
    weights[289:290, 0:48] = reduce_bv[...]
    kept[0:288, 0:C] = kept_v[...].reshape(288, C)
    sent[0:288, 0:C] = sent_v[...].reshape(288, C)
    for i in range(4):
        gains_out[i : i + 1, :] = gains_v[i].astype(F32)


def norm(x, gain, shift):
    mean = jnp.sum(x, axis=-1, keepdims=True) * (1.0 / C)
    centred = x - mean
    var = jnp.sum(centred * centred, axis=-1, keepdims=True) * (1.0 / C)
    return centred * lax.rsqrt(var + EPS) * gain + shift


def dot(a, b):
    return jnp.dot(a, b, preferred_element_type=F32)


def dot_t(a, b):
    return lax.dot_general(a, b, (((1,), (1,)), ((), ())), preferred_element_type=F32)


def assemble(pack, wqkv, wproj, wexp, wred, bqkv, brow):
    for j in range(4):
        wqkv[144 * j : 144 * (j + 1), :] = pack[j, 0:144, 0:192]
        wproj[48 * j : 48 * (j + 1), :] = pack[j, 144:192, 0:192]
        wexp[:, C * j : C * (j + 1)] = pack[j, 0:192, 192:384]
        wred[C * j : C * j + 96, :] = pack[j, 192:288, 0:192]
        wred[C * j + 96 : C * (j + 1), :] = pack[j, 192:288, 192:384]
        brow[0:1, C * j : C * (j + 1)] = pack[j, 288:289, 192:384].astype(F32)
        brow[1:2, 48 * j : 48 * (j + 1)] = pack[j, 288:289, 144:192].astype(F32)
        brow[2:3, 48 * j : 48 * (j + 1)] = pack[j, 289:290, 0:48].astype(F32)
        at = 144 * j
        while at < 144 * (j + 1):
            part, inner = divmod(at, C)
            size = min(C - inner, 144 * (j + 1) - at)
            source = at - 144 * j
            bqkv[part : part + 1, inner : inner + size] = pack[
                j, 288:289, source : source + size
            ].astype(F32)
            at += size


def expand_bias(fields, turn, bias):
    for half, field in enumerate(fields):
        parts = None
        for zk in range(WZ):
            rows = slice(288 + 144 * zk, 288 + 144 * (zk + 1))
            part = dot(field[rows, 0:SIDE], turn[SIDE * zk : SIDE * (zk + 1), :])
            parts = part if parts is None else parts + part
        turned = (parts[0:48] + parts[48:96] + parts[96:144]) * LOG2E
        for wq in range(WW):
            start = KEYS * (WW - 1 - wq)
            piece = turned[:, start : start + WIN]
            row = wq * KEYS + half * WZ * HALF
            for h in range(HEADS):
                bias[h, row : row + WZ * HALF, :] = piece[8 * h : 8 * h + WZ * HALF, :]


def attend(q, k, v, bias):
    head_of = lax.broadcasted_iota(jnp.int32, (WIN, C), 1) // DIM
    scale = LOG2E / float(np.sqrt(DIM))
    zero = jnp.zeros((WIN, C), BF)
    stacked = jnp.concatenate([jnp.where(head_of == h, q, zero) for h in range(HEADS)], axis=0)
    scores = dot_t(stacked, k)
    probs, inverse = [], []
    for h in range(HEADS):
        own = scores[WIN * h : WIN * (h + 1)] * scale + bias[h]
        weights = jnp.exp2(own - jnp.max(own, axis=-1, keepdims=True))
        inverse.append(1.0 / jnp.sum(weights, axis=-1, keepdims=True))
        probs.append(weights.astype(BF))
    values = dot(jnp.concatenate(probs, axis=0), v)
    total = values[0:WIN] * inverse[0]
    for h in range(1, HEADS):
        part = values[WIN * h : WIN * (h + 1)] * inverse[h]
        total = jnp.where(head_of == h, part, total)
    return total.astype(BF)


def block(x, gains, wqkv, wproj, wexp, wred, bqkv, brow, bias):
    floats = x.astype(F32)
    normed = norm(floats, gains[0:1, :], gains[1:2, :]).astype(BF)
    q, k, v = (
        (dot_t(normed, wqkv[C * i : C * (i + 1), :]) + bqkv[i : i + 1, :]).astype(BF)
        for i in range(3)
    )
    windows = (slice(WIN * w, WIN * (w + 1)) for w in range(2))
    attended = jnp.concatenate([attend(q[rows], k[rows], v[rows], bias) for rows in windows], axis=0)
    middle = (floats + dot_t(attended, wproj[...]) + brow[1:2, 0:C]).astype(BF)
    middle_floats = middle.astype(F32)
    normed_two = norm(middle_floats, gains[2:3, :], gains[3:4, :]).astype(BF)
    total = middle_floats + brow[2:3, 0:C]
    for at in range(0, MLP, 256):
        pre = dot(normed_two, wexp[:, at : at + 256]) + brow[0:1, at : at + 256]
        hidden = (0.5 * pre * (1.0 + lax.erf(pre * float(np.sqrt(0.5))))).astype(BF)
        total = total + dot(hidden, wred[at : at + 256, :])
    return total.astype(BF)


def daily_block(t, fields, pick, out, *rest):
    rows = slice(WIN * t, WIN * (t + 1))
    source = jnp.concatenate([field[rows, 0:C] for field in fields], axis=0)
    result = block(dot(pick[...], source).astype(BF), *rest)
    out[:, 0:C] = result[0:WIN]
    out[:, C : 2 * C] = result[WIN : 2 * WIN]


def prepare_kernel(own, other, pick, pack, gains, turn, out, bias, *mats):
    section = lax.axis_index("section")
    turn = turn.at[lax.rem(lax.axis_index("lat"), 2)]

    @pl.when(section == 0)
    def _():
        assemble(pack, *mats)
        expand_bias((own, other), turn, bias)
        daily_block(0, (own, other), pick, out, gains, *mats, bias)

    @pl.when(section == 1)
    def _():
        assemble(pack, *mats)
        expand_bias((own, other), turn, bias)


def daily_kernel(own, other, pick, gains, bias, *rest):
    *mats, out = rest

    @pl.when(lax.axis_index("section") == 0)
    def _():
        daily_block(1, (own, other), pick, out, gains, *mats, bias)


def chained_block(received, own, split, gains, bias, mats, hold):
    section = lax.axis_index("section")

    @pl.when(section == 0)
    def _():
        hold[0:WIN, :] = own[:, 0:C]
        hold[WIN : 2 * WIN, :] = own[:, C : 2 * C]

    @pl.when(section == 1)
    def _():
        hold[0:WIN, :] = received[:, 0:C]
        hold[WIN : 2 * WIN, :] = received[:, C : 2 * C]
        hold[...] = block(hold[...], gains, *mats, bias)

    ordered = dot(split[...], hold[...]).astype(BF)
    return ordered[0:WIN], ordered[WIN : 2 * WIN]


def chained_kernel(received, own, split, gains, bias, *rest):
    *mats, out, hold = rest
    out[0], out[1] = chained_block(received, own, split, gains, bias, mats, hold)


def last_kernel(earlier, received, own, split, gains, bias, *rest):
    *mats, out, hold = rest
    core = lax.rem(lax.axis_index("lat"), 2)
    halves = chained_block(received, own, split, gains, bias, mats, hold)
    for other in range(2):
        half = core if other == 0 else 1 - core
        out[half, 0] = earlier[other]
        out[half, 1] = halves[other]


def place_kernel(both, out, sems):
    core = lax.rem(lax.axis_index("lat"), 2)
    copies = [
        pltpu.make_async_copy(both.at[side, core], out.at[:, pl.ds(24 * side, 24), :], sems.at[side])
        for side in range(2)
    ]
    for copy in copies:
        copy.start()
    for copy in copies:
        copy.wait()


def call(kernel, out_shape, args, scratch=(), flops=0):
    many = isinstance(out_shape, tuple)
    return pl.pallas_call(
        kernel,
        out_shape=out_shape,
        in_specs=[VMEM] * len(args),
        out_specs=(VMEM,) * len(out_shape) if many else VMEM,
        scratch_shapes=list(scratch),
        compiler_params=PARAMS,
        cost_estimate=pl.CostEstimate(flops=flops, bytes_accessed=1 << 20, transcendentals=0),
    )(*args)


def on_device(
    initial_field,
    first_gain,
    first_shift,
    qkv_weight,
    qkv_bias,
    proj_weight,
    proj_bias,
    second_gain,
    second_shift,
    expand_weight,
    expand_bias_row,
    reduce_weight,
    reduce_bias,
    earth_bias,
):
    lat_count = lax.axis_size("lat")
    pairs = [[2 * i, 2 * i + 1] for i in range(lat_count // 2)]
    shape = jax.ShapeDtypeStruct
    hbm = pl.BlockSpec(memory_space=pltpu.HBM)
    operands = (
        jnp.swapaxes(qkv_weight, 1, 2),
        jnp.swapaxes(proj_weight, 1, 2),
        expand_weight,
        reduce_weight,
        qkv_bias,
        proj_bias,
        expand_bias_row,
        reduce_bias,
        initial_field.reshape(12, 48, C),
        earth_bias.reshape(HEADS, 1, -1),
        first_gain,
        first_shift,
        second_gain,
        second_shift,
    )
    pick = jnp.asarray(pick_rows())
    split = jnp.asarray(pick_rows().T)
    turn = jnp.asarray(turn_columns())
    weights, kept, sent, gains = pl.pallas_call(
        load_kernel,
        out_shape=(
            shape((304, 384), BF),
            shape((576, 256), BF),
            shape((576, 256), BF),
            shape((4, C), F32),
        ),
        in_specs=[hbm] * len(operands),
        out_specs=(VMEM,) * 4,
        scratch_shapes=[
            pltpu.VMEM((144, C), BF),
            pltpu.VMEM((48, C), BF),
            pltpu.VMEM((C, C), BF),
            pltpu.VMEM((C, C), BF),
            pltpu.VMEM((1, 144), BF),
            pltpu.VMEM((1, 48), BF),
            pltpu.VMEM((1, C), BF),
            pltpu.VMEM((1, 48), BF),
            pltpu.VMEM((12, 24, C), BF),
            pltpu.VMEM((12, 24, C), BF),
            pltpu.VMEM((8, 1656), F32),
            pltpu.VMEM((4, 1, C), BF),
            pltpu.VMEM((4, 48, 128), F32),
            pltpu.SemaphoreType.DMA((20,)),
        ],
        compiler_params=PARAMS,
    )(*(pltpu.with_memory_space_constraint(x, pltpu.HBM) for x in operands))
    swap = [(i, i ^ 1) for i in range(lat_count)]
    other = lax.ppermute(sent, "lat", swap)
    pack = lax.all_gather(weights, "tp")
    mats = (
        shape((3 * C, C), BF),
        shape((C, C), BF),
        shape((C, MLP), BF),
        shape((MLP, C), BF),
        shape((3, C), F32),
        shape((3, MLP), F32),
    )
    flops = 2 * 288 * 192 * 192 * 14
    dense = shape((WIN, 2 * C), BF)
    ahead = [(0, 1)]
    daily_0, bias, *mats = call(
        prepare_kernel,
        (dense, shape((HEADS, WIN, WIN), F32), *mats),
        (kept, other, pick, pack, gains, turn),
        flops=flops,
    )
    received_0 = lax.ppermute(daily_0, "section", ahead)
    daily_1 = call(
        daily_kernel, dense, (kept, other, pick, gains, bias, *mats), flops=flops
    )
    received_1 = lax.ppermute(daily_1, "section", ahead)
    hold = [pltpu.VMEM((2 * WIN, C), BF)]
    earlier = call(
        chained_kernel,
        shape((2, WIN, C), BF),
        (received_0, daily_0, split, gains, bias, *mats),
        hold,
        flops,
    )
    states = call(
        last_kernel,
        shape((2, 2, WIN, C), BF),
        (earlier, received_1, daily_1, split, gains, bias, *mats),
        hold,
        flops,
    )
    both = lax.all_gather(states, "lat", axis_index_groups=pairs)
    placed = pl.pallas_call(
        place_kernel,
        out_shape=shape((12, 48, C), BF),
        in_specs=[pl.BlockSpec(memory_space=pl.ANY)],
        out_specs=pl.BlockSpec(memory_space=pl.ANY),
        scratch_shapes=[pltpu.SemaphoreType.DMA((2,))],
        compiler_params=PARAMS,
    )(both.reshape(2, 2, 12, 24, C))
    return placed.reshape(1, 2, 2, 3, 48, C)


def solution(mesh):
    return jax.shard_map(
        on_device,
        mesh=mesh,
        in_specs=(
            P(None, "tp", "lat", None, None),
            P("section", None),
            P("section", None),
            P("section", None, "tp"),
            P("section", "tp"),
            P("section", None, "tp"),
            P("section", "tp"),
            P("section", None),
            P("section", None),
            P("section", None, "tp"),
            P("section", "tp"),
            P("section", "tp", None),
            P("section", "tp"),
            P("section", "tp", "lat", None, None),
        ),
        out_specs=P("section", None, "tp", "lat", None, None),
        check_vma=False,
    )
```

```python
import jax
import jax.numpy as jnp
import numpy as np
from jax import lax
from jax.experimental import pallas as pl
from jax.experimental.pallas import tpu as pltpu
from jax.sharding import PartitionSpec as P

WZ = 2
WH = 6
WW = 12
HALF = WH // 2
C = 192
HEADS = 6
DIM = C // HEADS
WIN = WZ * WH * WW
SPAN = 2 * WW - 1
KEYS = WZ * WH
LINE = KEYS * SPAN
MLP = 768
EPS = 1e-05
LOG2E = 1.4426950408889634
BF = jnp.bfloat16
F32 = jnp.float32
SIDE = WH * SPAN

VMEM = pl.BlockSpec(memory_space=pltpu.VMEM)
PARAMS = pltpu.CompilerParams(vmem_limit_bytes=20 * 1024 * 1024)


def places():
    row = 0
    for w in range(2):
        for wl in range(WW):
            for other in range(2):
                for z in range(WZ):
                    for h in range(HALF):
                        yield row, other, z, h, w * WW + wl
                        row += 1


def pick_rows():
    out = np.zeros((2 * WIN, 2 * WIN), np.float32)
    for row, other, z, h, lon in places():
        out[row, ((other * WZ + z) * HALF + h) * 24 + lon] = 1.0
    return out.astype(BF)


def turn_columns():
    out = np.zeros((2, LINE, LINE), np.float32)
    for core in range(2):
        for zk in range(WZ):
            for hk in range(WH):
                key = ((core ^ (hk // HALF)) * WZ + zk) * HALF + hk % HALF
                for j in range(SPAN):
                    out[core, (zk * WH + hk) * SPAN + j, (SPAN - 1 - j) * KEYS + key] = 1.0
    return out.astype(BF)


def load_kernel(
    qkv,
    proj,
    expand,
    reduce,
    qkv_b,
    proj_b,
    expand_b,
    reduce_b,
    field,
    table,
    g1,
    s1,
    g2,
    s2,
    weights,
    kept,
    sent,
    gains_out,
    qkv_v,
    proj_v,
    expand_v,
    reduce_v,
    qkv_bv,
    proj_bv,
    expand_bv,
    reduce_bv,
    kept_v,
    sent_v,
    table_v,
    gains_v,
    lines,
    sems,
):
    core = lax.rem(lax.axis_index("lat"), 2)
    moves = [(table.at[h], table_v.at[pl.ds(h, 1), :]) for h in range(HEADS)]
    moves += [
        (qkv.at[0], qkv_v),
        (proj.at[0], proj_v),
        (expand.at[0], expand_v),
        (reduce.at[0], reduce_v),
        (qkv_b, qkv_bv),
        (proj_b, proj_bv),
        (expand_b, expand_bv),
        (reduce_b, reduce_bv),
        (field.at[:, pl.ds(pl.multiple_of(24 * core, 8), 24), :], kept_v),
        (field.at[:, pl.ds(pl.multiple_of(24 - 24 * core, 8), 24), :], sent_v),
    ]
    moves += [(ref, gains_v.at[i]) for i, ref in enumerate((g1, s1, g2, s2))]
    copies = [pltpu.make_async_copy(a, b, sems.at[i]) for i, (a, b) in enumerate(moves)]
    for copy in copies:
        copy.start()
    weights[288:304, :] = jnp.zeros((16, 384), BF)
    lines[...] = jnp.zeros_like(lines)
    blank = jnp.zeros((HEADS, 256 - SIDE), F32)
    for copy in copies[:HEADS]:
        copy.wait()
    for zr in range(WZ * HALF):
        z, r = divmod(zr, HALF)
        for zk in range(WZ):
            start = ((z * WZ + zk) * HALF + r) * SIDE
            target = pl.ds(zr, HEADS, stride=8)
            lines[2 * zk, target, :] = table_v[0:HEADS, start : start + 128]
            tail = table_v[0:HEADS, start + 128 : start + SIDE]
            lines[2 * zk + 1, target, :] = jnp.concatenate([tail, blank], axis=1)
    for zk in range(WZ):
        whole = jnp.concatenate([lines[2 * zk], lines[2 * zk + 1]], axis=1)
        high = whole.astype(BF)
        rest = whole - high.astype(F32)
        middle = rest.astype(BF)
        low = (rest - middle.astype(F32)).astype(BF)
        for i, part in enumerate((high, middle, low)):
            rows = slice(288 + 144 * zk + 48 * i, 288 + 144 * zk + 48 * (i + 1))
            kept[rows, :] = part
            sent[rows, :] = part
    for copy in copies[HEADS:]:
        copy.wait()
    weights[0:144, 0:192] = qkv_v[...]
    weights[144:192, 0:192] = proj_v[...]
    weights[0:192, 192:384] = expand_v[...]
    weights[192:288, 0:192] = reduce_v[0:96, :]
    weights[192:288, 192:384] = reduce_v[96:192, :]
    weights[288:289, 0:144] = qkv_bv[...]
    weights[288:289, 144:192] = proj_bv[...]
    weights[288:289, 192:384] = expand_bv[...]
    weights[289:290, 0:48] = reduce_bv[...]
    kept[0:288, 0:C] = kept_v[...].reshape(288, C)
    sent[0:288, 0:C] = sent_v[...].reshape(288, C)
    for i in range(4):
        gains_out[i : i + 1, :] = gains_v[i].astype(F32)


def norm(x, gain, shift):
    mean = jnp.sum(x, axis=-1, keepdims=True) * (1.0 / C)
    centred = x - mean
    var = jnp.sum(centred * centred, axis=-1, keepdims=True) * (1.0 / C)
    return centred * lax.rsqrt(var + EPS) * gain + shift


def dot(a, b):
    return jnp.dot(a, b, preferred_element_type=F32)


def dot_t(a, b):
    return lax.dot_general(a, b, (((1,), (1,)), ((), ())), preferred_element_type=F32)


def assemble(pack, wqkv, wproj, wexp, wred, bqkv, brow):
    for j in range(4):
        wqkv[144 * j : 144 * (j + 1), :] = pack[j, 0:144, 0:192]
        wproj[48 * j : 48 * (j + 1), :] = pack[j, 144:192, 0:192]
        wexp[:, C * j : C * (j + 1)] = pack[j, 0:192, 192:384]
        wred[C * j : C * j + 96, :] = pack[j, 192:288, 0:192]
        wred[C * j + 96 : C * (j + 1), :] = pack[j, 192:288, 192:384]
        brow[0:1, C * j : C * (j + 1)] = pack[j, 288:289, 192:384].astype(F32)
        brow[1:2, 48 * j : 48 * (j + 1)] = pack[j, 288:289, 144:192].astype(F32)
        brow[2:3, 48 * j : 48 * (j + 1)] = pack[j, 289:290, 0:48].astype(F32)
        at = 144 * j
        while at < 144 * (j + 1):
            part, inner = divmod(at, C)
            size = min(C - inner, 144 * (j + 1) - at)
            source = at - 144 * j
            bqkv[part : part + 1, inner : inner + size] = pack[
                j, 288:289, source : source + size
            ].astype(F32)
            at += size


def expand_bias(fields, turn, bias):
    for half, field in enumerate(fields):
        parts = None
        for zk in range(WZ):
            rows = slice(288 + 144 * zk, 288 + 144 * (zk + 1))
            part = dot(field[rows, 0:SIDE], turn[SIDE * zk : SIDE * (zk + 1), :])
            parts = part if parts is None else parts + part
        turned = (parts[0:48] + parts[48:96] + parts[96:144]) * LOG2E
        for wq in range(WW):
            start = KEYS * (WW - 1 - wq)
            piece = turned[:, start : start + WIN]
            row = wq * KEYS + half * WZ * HALF
            for h in range(HEADS):
                bias[h, row : row + WZ * HALF, :] = piece[8 * h : 8 * h + WZ * HALF, :]


def attend(q, k, v, bias):
    head_of = lax.broadcasted_iota(jnp.int32, (WIN, C), 1) // DIM
    scale = LOG2E / float(np.sqrt(DIM))
    zero = jnp.zeros((WIN, C), BF)
    stacked = jnp.concatenate([jnp.where(head_of == h, q, zero) for h in range(HEADS)], axis=0)
    scores = dot_t(stacked, k)
    probs, inverse = [], []
    for h in range(HEADS):
        own = scores[WIN * h : WIN * (h + 1)] * scale + bias[h]
        weights = jnp.exp2(own - jnp.max(own, axis=-1, keepdims=True))
        inverse.append(1.0 / jnp.sum(weights, axis=-1, keepdims=True))
        probs.append(weights.astype(BF))
    values = dot(jnp.concatenate(probs, axis=0), v)
    total = values[0:WIN] * inverse[0]
    for h in range(1, HEADS):
        part = values[WIN * h : WIN * (h + 1)] * inverse[h]
        total = jnp.where(head_of == h, part, total)
    return total.astype(BF)


def block(x, gains, wqkv, wproj, wexp, wred, bqkv, brow, bias):
    floats = x.astype(F32)
    normed = norm(floats, gains[0:1, :], gains[1:2, :]).astype(BF)
    q, k, v = (
        (dot_t(normed, wqkv[C * i : C * (i + 1), :]) + bqkv[i : i + 1, :]).astype(BF)
        for i in range(3)
    )
    windows = (slice(at, at + WIN) for at in range(0, x.shape[0], WIN))
    attended = jnp.concatenate([attend(q[rows], k[rows], v[rows], bias) for rows in windows], axis=0)
    middle = (floats + dot_t(attended, wproj[...]) + brow[1:2, 0:C]).astype(BF)
    middle_floats = middle.astype(F32)
    normed_two = norm(middle_floats, gains[2:3, :], gains[3:4, :]).astype(BF)
    total = middle_floats + brow[2:3, 0:C]
    for at in range(0, MLP, 256):
        pre = dot(normed_two, wexp[:, at : at + 256]) + brow[0:1, at : at + 256]
        hidden = (0.5 * pre * (1.0 + lax.erf(pre * float(np.sqrt(0.5))))).astype(BF)
        total = total + dot(hidden, wred[at : at + 256, :])
    return total.astype(BF)


def daily_kernel(own, other, pick, pack, gains, turn, out, bias, *mats):
    assemble(pack, *mats)
    expand_bias((own, other), turn.at[lax.rem(lax.axis_index("lat"), 2)], bias)

    @pl.when(lax.axis_index("section") == 0)
    def _():
        tokens = []
        for t in range(2):
            rows = slice(WIN * t, WIN * (t + 1))
            source = jnp.concatenate([own[rows, 0:C], other[rows, 0:C]], axis=0)
            tokens.append(dot(pick[...], source).astype(BF))
        result = block(jnp.concatenate(tokens, axis=0), gains, *mats, bias)
        out[:, 0:C] = result[0 : 2 * WIN]
        out[:, C : 2 * C] = result[2 * WIN : 4 * WIN]


def chained_kernel(received, own, split, gains, bias, *rest):
    *mats, out, hold = rest
    section = lax.axis_index("section")
    core = lax.rem(lax.axis_index("lat"), 2)

    @pl.when(section == 0)
    def _():
        hold[0, ...] = own[:, 0:C]
        hold[1, ...] = own[:, C : 2 * C]

    @pl.when(section == 1)
    def _():
        x = jnp.concatenate([received[:, 0:C], received[:, C : 2 * C]], axis=0)
        result = block(x, gains, *mats, bias)
        hold[0, ...] = result[0 : 2 * WIN]
        hold[1, ...] = result[2 * WIN : 4 * WIN]

    for t in range(2):
        ordered = dot(split[...], hold[t]).astype(BF)
        out[core, t] = ordered[0:WIN]
        out[1 - core, t] = ordered[WIN : 2 * WIN]


def place_kernel(both, out, sems):
    core = lax.rem(lax.axis_index("lat"), 2)
    copies = [
        pltpu.make_async_copy(both.at[side, core], out.at[:, pl.ds(24 * side, 24), :], sems.at[side])
        for side in range(2)
    ]
    for copy in copies:
        copy.start()
    for copy in copies:
        copy.wait()


def call(kernel, out_shape, args, scratch=(), flops=0):
    many = isinstance(out_shape, tuple)
    return pl.pallas_call(
        kernel,
        out_shape=out_shape,
        in_specs=[VMEM] * len(args),
        out_specs=(VMEM,) * len(out_shape) if many else VMEM,
        scratch_shapes=list(scratch),
        compiler_params=PARAMS,
        cost_estimate=pl.CostEstimate(flops=flops, bytes_accessed=1 << 20, transcendentals=0),
    )(*args)


def on_device(
    initial_field,
    first_gain,
    first_shift,
    qkv_weight,
    qkv_bias,
    proj_weight,
    proj_bias,
    second_gain,
    second_shift,
    expand_weight,
    expand_bias_row,
    reduce_weight,
    reduce_bias,
    earth_bias,
):
    lat_count = lax.axis_size("lat")
    pairs = [[2 * i, 2 * i + 1] for i in range(lat_count // 2)]
    shape = jax.ShapeDtypeStruct
    hbm = pl.BlockSpec(memory_space=pltpu.HBM)
    operands = (
        jnp.swapaxes(qkv_weight, 1, 2),
        jnp.swapaxes(proj_weight, 1, 2),
        expand_weight,
        reduce_weight,
        qkv_bias,
        proj_bias,
        expand_bias_row,
        reduce_bias,
        initial_field.reshape(12, 48, C),
        earth_bias.reshape(HEADS, 1, -1),
        first_gain,
        first_shift,
        second_gain,
        second_shift,
    )
    pick = jnp.asarray(pick_rows())
    split = jnp.asarray(pick_rows().T)
    turn = jnp.asarray(turn_columns())
    weights, kept, sent, gains = pl.pallas_call(
        load_kernel,
        out_shape=(
            shape((304, 384), BF),
            shape((576, 256), BF),
            shape((576, 256), BF),
            shape((4, C), F32),
        ),
        in_specs=[hbm] * len(operands),
        out_specs=(VMEM,) * 4,
        scratch_shapes=[
            pltpu.VMEM((144, C), BF),
            pltpu.VMEM((48, C), BF),
            pltpu.VMEM((C, C), BF),
            pltpu.VMEM((C, C), BF),
            pltpu.VMEM((1, 144), BF),
            pltpu.VMEM((1, 48), BF),
            pltpu.VMEM((1, C), BF),
            pltpu.VMEM((1, 48), BF),
            pltpu.VMEM((12, 24, C), BF),
            pltpu.VMEM((12, 24, C), BF),
            pltpu.VMEM((8, 1656), F32),
            pltpu.VMEM((4, 1, C), BF),
            pltpu.VMEM((4, 48, 128), F32),
            pltpu.SemaphoreType.DMA((20,)),
        ],
        compiler_params=PARAMS,
    )(*(pltpu.with_memory_space_constraint(x, pltpu.HBM) for x in operands))
    swap = [(i, i ^ 1) for i in range(lat_count)]
    other = lax.ppermute(sent, "lat", swap)
    pack = lax.all_gather(weights, "tp")
    mats = (
        shape((3 * C, C), BF),
        shape((C, C), BF),
        shape((C, MLP), BF),
        shape((MLP, C), BF),
        shape((3, C), F32),
        shape((3, MLP), F32),
    )
    flops = 2 * 576 * 192 * 192 * 14
    daily, bias, *mats = call(
        daily_kernel,
        (shape((2 * WIN, 2 * C), BF), shape((HEADS, WIN, WIN), F32), *mats),
        (kept, other, pick, pack, gains, turn),
        flops=flops,
    )
    received = lax.ppermute(daily, "section", [(0, 1)])
    states = call(
        chained_kernel,
        shape((2, 2, WIN, C), BF),
        (received, daily, split, gains, bias, *mats),
        [pltpu.VMEM((2, 2 * WIN, C), BF)],
        flops,
    )
    both = lax.all_gather(states, "lat", axis_index_groups=pairs)
    placed = pl.pallas_call(
        place_kernel,
        out_shape=shape((12, 48, C), BF),
        in_specs=[pl.BlockSpec(memory_space=pl.ANY)],
        out_specs=pl.BlockSpec(memory_space=pl.ANY),
        scratch_shapes=[pltpu.SemaphoreType.DMA((2,))],
        compiler_params=PARAMS,
    )(both.reshape(2, 2, 12, 24, C))
    return placed.reshape(1, 2, 2, 3, 48, C)


def solution(mesh):
    return jax.shard_map(
        on_device,
        mesh=mesh,
        in_specs=(
            P(None, "tp", "lat", None, None),
            P("section", None),
            P("section", None),
            P("section", None, "tp"),
            P("section", "tp"),
            P("section", None, "tp"),
            P("section", "tp"),
            P("section", None),
            P("section", None),
            P("section", None, "tp"),
            P("section", "tp"),
            P("section", "tp", None),
            P("section", "tp"),
            P("section", "tp", "lat", None, None),
        ),
        out_specs=P("section", None, "tp", "lat", None, None),
        check_vma=False,
    )
```

```python
import jax
import jax.numpy as jnp
import numpy as np
from jax import lax
from jax.experimental import pallas as pl
from jax.experimental.pallas import tpu as pltpu
from jax.sharding import PartitionSpec as P

WZ = 2
WH = 6
WW = 12
HALF = WH // 2
C = 192
HEADS = 6
DIM = C // HEADS
WIN = WZ * WH * WW
SPAN = 2 * WW - 1
KEYS = WZ * WH
LINE = KEYS * SPAN
MLP = 768
EPS = 1e-05
LOG2E = 1.4426950408889634
BF = jnp.bfloat16
F32 = jnp.float32
SIDE = WH * SPAN

VMEM = pl.BlockSpec(memory_space=pltpu.VMEM)
PARAMS = pltpu.CompilerParams(vmem_limit_bytes=20 * 1024 * 1024)


def places():
    row = 0
    for w in range(2):
        for wl in range(WW):
            for other in range(2):
                for z in range(WZ):
                    for h in range(HALF):
                        yield row, other, z, h, w * WW + wl
                        row += 1


def pick_rows():
    out = np.zeros((2 * WIN, 2 * WIN), np.float32)
    for row, other, z, h, lon in places():
        out[row, ((other * WZ + z) * HALF + h) * 24 + lon] = 1.0
    return out.astype(BF)


def turn_columns():
    out = np.zeros((2, LINE, LINE), np.float32)
    for core in range(2):
        for zk in range(WZ):
            for hk in range(WH):
                key = ((core ^ (hk // HALF)) * WZ + zk) * HALF + hk % HALF
                for j in range(SPAN):
                    out[core, (zk * WH + hk) * SPAN + j, (SPAN - 1 - j) * KEYS + key] = 1.0
    return out.astype(BF)


def load_kernel(
    qkv,
    proj,
    expand,
    reduce,
    qkv_b,
    proj_b,
    expand_b,
    reduce_b,
    field,
    table,
    g1,
    s1,
    g2,
    s2,
    weights,
    kept,
    sent,
    gains_out,
    qkv_v,
    proj_v,
    expand_v,
    reduce_v,
    qkv_bv,
    proj_bv,
    expand_bv,
    reduce_bv,
    kept_v,
    sent_v,
    table_v,
    gains_v,
    lines,
    sems,
):
    core = lax.rem(lax.axis_index("lat"), 2)
    moves = [(table.at[h], table_v.at[pl.ds(h, 1), :]) for h in range(HEADS)]
    moves += [
        (field.at[:, pl.ds(pl.multiple_of(24 * core, 8), 24), :], kept_v),
        (field.at[:, pl.ds(pl.multiple_of(24 - 24 * core, 8), 24), :], sent_v),
        (expand.at[0], expand_v),
        (reduce.at[0], reduce_v),
        (qkv.at[0], qkv_v),
        (proj.at[0], proj_v),
        (qkv_b, qkv_bv),
        (proj_b, proj_bv),
        (expand_b, expand_bv),
        (reduce_b, reduce_bv),
    ]
    moves += [(ref, gains_v.at[i]) for i, ref in enumerate((g1, s1, g2, s2))]
    copies = [pltpu.make_async_copy(a, b, sems.at[i]) for i, (a, b) in enumerate(moves)]
    for copy in copies:
        copy.start()
    weights[288:304, :] = jnp.zeros((16, 384), BF)
    lines[...] = jnp.zeros_like(lines)
    blank = jnp.zeros((HEADS, 256 - SIDE), F32)
    for copy in copies[:HEADS]:
        copy.wait()
    for zr in range(WZ * HALF):
        z, r = divmod(zr, HALF)
        for zk in range(WZ):
            start = ((z * WZ + zk) * HALF + r) * SIDE
            target = pl.ds(zr, HEADS, stride=8)
            lines[2 * zk, target, :] = table_v[0:HEADS, start : start + 128]
            tail = table_v[0:HEADS, start + 128 : start + SIDE]
            lines[2 * zk + 1, target, :] = jnp.concatenate([tail, blank], axis=1)
    for zk in range(WZ):
        whole = jnp.concatenate([lines[2 * zk], lines[2 * zk + 1]], axis=1)
        high = whole.astype(BF)
        rest = whole - high.astype(F32)
        middle = rest.astype(BF)
        low = (rest - middle.astype(F32)).astype(BF)
        for i, part in enumerate((high, middle, low)):
            rows = slice(288 + 144 * zk + 48 * i, 288 + 144 * zk + 48 * (i + 1))
            kept[rows, :] = part
            sent[rows, :] = part
    arrived = iter(copies[HEADS:])
    next(arrived).wait()
    kept[0:288, 0:C] = kept_v[...].reshape(288, C)
    next(arrived).wait()
    sent[0:288, 0:C] = sent_v[...].reshape(288, C)
    next(arrived).wait()
    weights[0:192, 192:384] = expand_v[...]
    next(arrived).wait()
    weights[192:288, 0:192] = reduce_v[0:96, :]
    weights[192:288, 192:384] = reduce_v[96:192, :]
    next(arrived).wait()
    weights[0:144, 0:192] = qkv_v[...]
    next(arrived).wait()
    weights[144:192, 0:192] = proj_v[...]
    for copy in arrived:
        copy.wait()
    weights[288:289, 0:144] = qkv_bv[...]
    weights[288:289, 144:192] = proj_bv[...]
    weights[288:289, 192:384] = expand_bv[...]
    weights[289:290, 0:48] = reduce_bv[...]
    for i in range(4):
        gains_out[i : i + 1, :] = gains_v[i].astype(F32)


def norm(x, gain, shift):
    mean = jnp.sum(x, axis=-1, keepdims=True) * (1.0 / C)
    centred = x - mean
    var = jnp.sum(centred * centred, axis=-1, keepdims=True) * (1.0 / C)
    return centred * lax.rsqrt(var + EPS) * gain + shift


def dot(a, b):
    return jnp.dot(a, b, preferred_element_type=F32)


def dot_t(a, b):
    return lax.dot_general(a, b, (((1,), (1,)), ((), ())), preferred_element_type=F32)


def assemble(pack, wqkv, wproj, wexp, wred, bqkv, brow):
    for j in range(4):
        wqkv[144 * j : 144 * (j + 1), :] = pack[j, 0:144, 0:192]
        wproj[48 * j : 48 * (j + 1), :] = pack[j, 144:192, 0:192]
        wexp[:, C * j : C * (j + 1)] = pack[j, 0:192, 192:384]
        wred[C * j : C * j + 96, :] = pack[j, 192:288, 0:192]
        wred[C * j + 96 : C * (j + 1), :] = pack[j, 192:288, 192:384]
        brow[0:1, C * j : C * (j + 1)] = pack[j, 288:289, 192:384].astype(F32)
        brow[1:2, 48 * j : 48 * (j + 1)] = pack[j, 288:289, 144:192].astype(F32)
        brow[2:3, 48 * j : 48 * (j + 1)] = pack[j, 289:290, 0:48].astype(F32)
        at = 144 * j
        while at < 144 * (j + 1):
            part, inner = divmod(at, C)
            size = min(C - inner, 144 * (j + 1) - at)
            source = at - 144 * j
            bqkv[part : part + 1, inner : inner + size] = pack[
                j, 288:289, source : source + size
            ].astype(F32)
            at += size


def expand_bias(fields, turn, bias):
    for half, field in enumerate(fields):
        parts = None
        for zk in range(WZ):
            rows = slice(288 + 144 * zk, 288 + 144 * (zk + 1))
            part = dot(field[rows, 0:SIDE], turn[SIDE * zk : SIDE * (zk + 1), :])
            parts = part if parts is None else parts + part
        turned = (parts[0:48] + parts[48:96] + parts[96:144]) * LOG2E
        for wq in range(WW):
            start = KEYS * (WW - 1 - wq)
            piece = turned[:, start : start + WIN]
            row = wq * KEYS + half * WZ * HALF
            for h in range(HEADS):
                bias[h, row : row + WZ * HALF, :] = piece[8 * h : 8 * h + WZ * HALF, :]


def attend(q, k, v, bias):
    head_of = lax.broadcasted_iota(jnp.int32, (WIN, C), 1) // DIM
    scale = LOG2E / float(np.sqrt(DIM))
    zero = jnp.zeros((WIN, C), BF)
    stacked = jnp.concatenate([jnp.where(head_of == h, q, zero) for h in range(HEADS)], axis=0)
    scores = dot_t(stacked, k)
    probs, inverse = [], []
    for h in range(HEADS):
        own = scores[WIN * h : WIN * (h + 1)] * scale + bias[h]
        weights = jnp.exp2(own - jnp.max(own, axis=-1, keepdims=True))
        inverse.append(1.0 / jnp.sum(weights, axis=-1, keepdims=True))
        probs.append(weights.astype(BF))
    values = dot(jnp.concatenate(probs, axis=0), v)
    total = values[0:WIN] * inverse[0]
    for h in range(1, HEADS):
        part = values[WIN * h : WIN * (h + 1)] * inverse[h]
        total = jnp.where(head_of == h, part, total)
    return total.astype(BF)


def block(x, gains, wqkv, wproj, wexp, wred, bqkv, brow, bias):
    floats = x.astype(F32)
    normed = norm(floats, gains[0:1, :], gains[1:2, :]).astype(BF)
    q, k, v = (
        (dot_t(normed, wqkv[C * i : C * (i + 1), :]) + bqkv[i : i + 1, :]).astype(BF)
        for i in range(3)
    )
    windows = (slice(at, at + WIN) for at in range(0, x.shape[0], WIN))
    attended = jnp.concatenate([attend(q[rows], k[rows], v[rows], bias) for rows in windows], axis=0)
    middle = (floats + dot_t(attended, wproj[...]) + brow[1:2, 0:C]).astype(BF)
    middle_floats = middle.astype(F32)
    normed_two = norm(middle_floats, gains[2:3, :], gains[3:4, :]).astype(BF)
    total = middle_floats + brow[2:3, 0:C]
    for at in range(0, MLP, 256):
        pre = dot(normed_two, wexp[:, at : at + 256]) + brow[0:1, at : at + 256]
        hidden = (0.5 * pre * (1.0 + lax.erf(pre * float(np.sqrt(0.5))))).astype(BF)
        total = total + dot(hidden, wred[at : at + 256, :])
    return total.astype(BF)


def daily_kernel(own, other, pick, pack, gains, turn, out_0, out_1, bias, *mats):
    assemble(pack, *mats)
    expand_bias((own, other), turn.at[lax.rem(lax.axis_index("lat"), 2)], bias)

    @pl.when(lax.axis_index("section") == 0)
    def _():
        tokens = []
        for t in range(2):
            rows = slice(WIN * t, WIN * (t + 1))
            source = jnp.concatenate([own[rows, 0:C], other[rows, 0:C]], axis=0)
            tokens.append(dot(pick[...], source).astype(BF))
        result = block(jnp.concatenate(tokens, axis=0), gains, *mats, bias)
        for w, (out, side) in enumerate(((out_0, 0), (out_0, C), (out_1, 0), (out_1, C))):
            out[:, side : side + C] = result[WIN * w : WIN * (w + 1)]


def chained_block(received, own, split, gains, bias, mats, hold):
    section = lax.axis_index("section")

    @pl.when(section == 0)
    def _():
        hold[0:WIN, :] = own[:, 0:C]
        hold[WIN : 2 * WIN, :] = own[:, C : 2 * C]

    @pl.when(section == 1)
    def _():
        x = jnp.concatenate([received[:, 0:C], received[:, C : 2 * C]], axis=0)
        hold[...] = block(x, gains, *mats, bias)

    ordered = dot(split[...], hold[...]).astype(BF)
    return ordered[0:WIN], ordered[WIN : 2 * WIN]


def chained_kernel(received, own, split, gains, bias, *rest):
    *mats, out, hold = rest
    out[0], out[1] = chained_block(received, own, split, gains, bias, mats, hold)


def last_kernel(earlier, received, own, split, gains, bias, *rest):
    *mats, out, hold = rest
    core = lax.rem(lax.axis_index("lat"), 2)
    out[core, 0] = earlier[0]
    out[1 - core, 0] = earlier[1]
    mine, theirs = chained_block(received, own, split, gains, bias, mats, hold)
    out[core, 1] = mine
    out[1 - core, 1] = theirs


def place_kernel(both, out, sems):
    core = lax.rem(lax.axis_index("lat"), 2)
    copies = [
        pltpu.make_async_copy(both.at[side, core], out.at[:, pl.ds(24 * side, 24), :], sems.at[side])
        for side in range(2)
    ]
    for copy in copies:
        copy.start()
    for copy in copies:
        copy.wait()


def call(kernel, out_shape, args, scratch=(), flops=0):
    many = isinstance(out_shape, tuple)
    return pl.pallas_call(
        kernel,
        out_shape=out_shape,
        in_specs=[VMEM] * len(args),
        out_specs=(VMEM,) * len(out_shape) if many else VMEM,
        scratch_shapes=list(scratch),
        compiler_params=PARAMS,
        cost_estimate=pl.CostEstimate(flops=flops, bytes_accessed=1 << 20, transcendentals=0),
    )(*args)


def on_device(
    initial_field,
    first_gain,
    first_shift,
    qkv_weight,
    qkv_bias,
    proj_weight,
    proj_bias,
    second_gain,
    second_shift,
    expand_weight,
    expand_bias_row,
    reduce_weight,
    reduce_bias,
    earth_bias,
):
    lat_count = lax.axis_size("lat")
    pairs = [[2 * i, 2 * i + 1] for i in range(lat_count // 2)]
    shape = jax.ShapeDtypeStruct
    hbm = pl.BlockSpec(memory_space=pltpu.HBM)
    operands = (
        jnp.swapaxes(qkv_weight, 1, 2),
        jnp.swapaxes(proj_weight, 1, 2),
        expand_weight,
        reduce_weight,
        qkv_bias,
        proj_bias,
        expand_bias_row,
        reduce_bias,
        initial_field.reshape(12, 48, C),
        earth_bias.reshape(HEADS, 1, -1),
        first_gain,
        first_shift,
        second_gain,
        second_shift,
    )
    pick = jnp.asarray(pick_rows())
    split = jnp.asarray(pick_rows().T)
    turn = jnp.asarray(turn_columns())
    weights, kept, sent, gains = pl.pallas_call(
        load_kernel,
        out_shape=(
            shape((304, 384), BF),
            shape((576, 256), BF),
            shape((576, 256), BF),
            shape((4, C), F32),
        ),
        in_specs=[hbm] * len(operands),
        out_specs=(VMEM,) * 4,
        scratch_shapes=[
            pltpu.VMEM((144, C), BF),
            pltpu.VMEM((48, C), BF),
            pltpu.VMEM((C, C), BF),
            pltpu.VMEM((C, C), BF),
            pltpu.VMEM((1, 144), BF),
            pltpu.VMEM((1, 48), BF),
            pltpu.VMEM((1, C), BF),
            pltpu.VMEM((1, 48), BF),
            pltpu.VMEM((12, 24, C), BF),
            pltpu.VMEM((12, 24, C), BF),
            pltpu.VMEM((8, 1656), F32),
            pltpu.VMEM((4, 1, C), BF),
            pltpu.VMEM((4, 48, 128), F32),
            pltpu.SemaphoreType.DMA((20,)),
        ],
        compiler_params=PARAMS,
    )(*(pltpu.with_memory_space_constraint(x, pltpu.HBM) for x in operands))
    swap = [(i, i ^ 1) for i in range(lat_count)]
    other = lax.ppermute(sent, "lat", swap)
    pack = lax.all_gather(weights, "tp")
    mats = (
        shape((3 * C, C), BF),
        shape((C, C), BF),
        shape((C, MLP), BF),
        shape((MLP, C), BF),
        shape((3, C), F32),
        shape((3, MLP), F32),
    )
    flops = 2 * 576 * 192 * 192 * 14
    dense = shape((WIN, 2 * C), BF)
    daily_0, daily_1, bias, *mats = call(
        daily_kernel,
        (dense, dense, shape((HEADS, WIN, WIN), F32), *mats),
        (kept, other, pick, pack, gains, turn),
        flops=flops,
    )
    received_0 = lax.ppermute(daily_0, "section", [(0, 1)])
    received_1 = lax.ppermute(daily_1, "section", [(0, 1)])
    hold = [pltpu.VMEM((2 * WIN, C), BF)]
    shared = (split, gains, bias, *mats)
    earlier = call(
        chained_kernel,
        shape((2, WIN, C), BF),
        (received_0, daily_0, *shared),
        hold,
        flops // 2,
    )
    states = call(
        last_kernel,
        shape((2, 2, WIN, C), BF),
        (earlier, received_1, daily_1, *shared),
        hold,
        flops // 2,
    )
    both = lax.all_gather(states, "lat", axis_index_groups=pairs)
    placed = pl.pallas_call(
        place_kernel,
        out_shape=shape((12, 48, C), BF),
        in_specs=[pl.BlockSpec(memory_space=pl.ANY)],
        out_specs=pl.BlockSpec(memory_space=pl.ANY),
        scratch_shapes=[pltpu.SemaphoreType.DMA((2,))],
        compiler_params=PARAMS,
    )(both.reshape(2, 2, 12, 24, C))
    return placed.reshape(1, 2, 2, 3, 48, C)


def solution(mesh):
    return jax.shard_map(
        on_device,
        mesh=mesh,
        in_specs=(
            P(None, "tp", "lat", None, None),
            P("section", None),
            P("section", None),
            P("section", None, "tp"),
            P("section", "tp"),
            P("section", None, "tp"),
            P("section", "tp"),
            P("section", None),
            P("section", None),
            P("section", None, "tp"),
            P("section", "tp"),
            P("section", "tp", None),
            P("section", "tp"),
            P("section", "tp", "lat", None, None),
        ),
        out_specs=P("section", None, "tp", "lat", None, None),
        check_vma=False,
    )
```

```python
import jax
import jax.numpy as jnp
import numpy as np
from jax import lax
from jax.experimental import pallas as pl
from jax.experimental.pallas import tpu as pltpu
from jax.sharding import PartitionSpec as P

WZ = 2
WH = 6
WW = 12
HALF = WH // 2
C = 192
HEADS = 6
DIM = C // HEADS
WIN = WZ * WH * WW
SPAN = 2 * WW - 1
KEYS = WZ * WH
LINE = KEYS * SPAN
MLP = 768
EPS = 1e-05
LOG2E = 1.4426950408889634
BF = jnp.bfloat16
F32 = jnp.float32
SIDE = WH * SPAN

VMEM = pl.BlockSpec(memory_space=pltpu.VMEM)
PARAMS = pltpu.CompilerParams(vmem_limit_bytes=20 * 1024 * 1024)


def places():
    row = 0
    for w in range(2):
        for wl in range(WW):
            for other in range(2):
                for z in range(WZ):
                    for h in range(HALF):
                        yield row, other, z, h, w * WW + wl
                        row += 1


def pick_rows():
    out = np.zeros((2 * WIN, 2 * WIN), np.float32)
    for row, other, z, h, lon in places():
        out[row, ((other * WZ + z) * HALF + h) * 24 + lon] = 1.0
    return out.astype(BF)


def turn_columns():
    out = np.zeros((2, LINE, LINE), np.float32)
    for core in range(2):
        for zk in range(WZ):
            for hk in range(WH):
                key = ((core ^ (hk // HALF)) * WZ + zk) * HALF + hk % HALF
                for j in range(SPAN):
                    out[core, (zk * WH + hk) * SPAN + j, (SPAN - 1 - j) * KEYS + key] = 1.0
    return out.astype(BF)


def load_kernel(
    qkv,
    proj,
    expand,
    reduce,
    qkv_b,
    proj_b,
    expand_b,
    reduce_b,
    field,
    table,
    g1,
    s1,
    g2,
    s2,
    weights,
    kept,
    sent,
    gains_out,
    qkv_v,
    proj_v,
    expand_v,
    reduce_v,
    qkv_bv,
    proj_bv,
    expand_bv,
    reduce_bv,
    kept_v,
    sent_v,
    table_v,
    gains_v,
    lines,
    sems,
):
    core = lax.rem(lax.axis_index("lat"), 2)
    moves = [(table.at[h], table_v.at[pl.ds(h, 1), :]) for h in range(HEADS)]
    moves += [
        (field.at[:, pl.ds(pl.multiple_of(24 * core, 8), 24), :], kept_v),
        (field.at[:, pl.ds(pl.multiple_of(24 - 24 * core, 8), 24), :], sent_v),
        (expand.at[0], expand_v),
        (reduce.at[0], reduce_v),
        (qkv.at[0], qkv_v),
        (proj.at[0], proj_v),
        (qkv_b, qkv_bv),
        (proj_b, proj_bv),
        (expand_b, expand_bv),
        (reduce_b, reduce_bv),
    ]
    moves += [(ref, gains_v.at[i]) for i, ref in enumerate((g1, s1, g2, s2))]
    copies = [pltpu.make_async_copy(a, b, sems.at[i]) for i, (a, b) in enumerate(moves)]
    for copy in copies:
        copy.start()
    weights[288:304, :] = jnp.zeros((16, 384), BF)
    lines[...] = jnp.zeros_like(lines)
    blank = jnp.zeros((HEADS, 256 - SIDE), F32)
    for copy in copies[:HEADS]:
        copy.wait()
    for zr in range(WZ * HALF):
        z, r = divmod(zr, HALF)
        for zk in range(WZ):
            start = ((z * WZ + zk) * HALF + r) * SIDE
            target = pl.ds(zr, HEADS, stride=8)
            lines[2 * zk, target, :] = table_v[0:HEADS, start : start + 128]
            tail = table_v[0:HEADS, start + 128 : start + SIDE]
            lines[2 * zk + 1, target, :] = jnp.concatenate([tail, blank], axis=1)
    for zk in range(WZ):
        whole = jnp.concatenate([lines[2 * zk], lines[2 * zk + 1]], axis=1)
        high = whole.astype(BF)
        rest = whole - high.astype(F32)
        middle = rest.astype(BF)
        low = (rest - middle.astype(F32)).astype(BF)
        for i, part in enumerate((high, middle, low)):
            rows = slice(288 + 144 * zk + 48 * i, 288 + 144 * zk + 48 * (i + 1))
            kept[rows, :] = part
            sent[rows, :] = part
    arrived = iter(copies[HEADS:])
    next(arrived).wait()
    kept[0:288, 0:C] = kept_v[...].reshape(288, C)
    next(arrived).wait()
    sent[0:288, 0:C] = sent_v[...].reshape(288, C)
    next(arrived).wait()
    weights[0:192, 192:384] = expand_v[...]
    next(arrived).wait()
    weights[192:288, 0:192] = reduce_v[0:96, :]
    weights[192:288, 192:384] = reduce_v[96:192, :]
    next(arrived).wait()
    weights[0:144, 0:192] = qkv_v[...]
    next(arrived).wait()
    weights[144:192, 0:192] = proj_v[...]
    for copy in arrived:
        copy.wait()
    weights[288:289, 0:144] = qkv_bv[...]
    weights[288:289, 144:192] = proj_bv[...]
    weights[288:289, 192:384] = expand_bv[...]
    weights[289:290, 0:48] = reduce_bv[...]
    for i in range(4):
        gains_out[i : i + 1, :] = gains_v[i].astype(F32)


def norm(x, gain, shift):
    mean = jnp.sum(x, axis=-1, keepdims=True) * (1.0 / C)
    centred = x - mean
    var = jnp.sum(centred * centred, axis=-1, keepdims=True) * (1.0 / C)
    return centred * lax.rsqrt(var + EPS) * gain + shift


def dot(a, b):
    return jnp.dot(a, b, preferred_element_type=F32)


def dot_t(a, b):
    return lax.dot_general(a, b, (((1,), (1,)), ((), ())), preferred_element_type=F32)


def assemble(pack, wqkv, wproj, wexp, wred, bqkv, brow):
    for j in range(4):
        wqkv[144 * j : 144 * (j + 1), :] = pack[j, 0:144, 0:192]
        wproj[48 * j : 48 * (j + 1), :] = pack[j, 144:192, 0:192]
        wexp[:, C * j : C * (j + 1)] = pack[j, 0:192, 192:384]
        wred[C * j : C * j + 96, :] = pack[j, 192:288, 0:192]
        wred[C * j + 96 : C * (j + 1), :] = pack[j, 192:288, 192:384]
        brow[0:1, C * j : C * (j + 1)] = pack[j, 288:289, 192:384].astype(F32)
        brow[1:2, 48 * j : 48 * (j + 1)] = pack[j, 288:289, 144:192].astype(F32)
        brow[2:3, 48 * j : 48 * (j + 1)] = pack[j, 289:290, 0:48].astype(F32)
        at = 144 * j
        while at < 144 * (j + 1):
            part, inner = divmod(at, C)
            size = min(C - inner, 144 * (j + 1) - at)
            source = at - 144 * j
            bqkv[part : part + 1, inner : inner + size] = pack[
                j, 288:289, source : source + size
            ].astype(F32)
            at += size


def expand_bias(fields, turn, bias):
    for half, field in enumerate(fields):
        parts = None
        for zk in range(WZ):
            rows = slice(288 + 144 * zk, 288 + 144 * (zk + 1))
            part = dot(field[rows, 0:SIDE], turn[SIDE * zk : SIDE * (zk + 1), :])
            parts = part if parts is None else parts + part
        turned = (parts[0:48] + parts[48:96] + parts[96:144]) * LOG2E
        for wq in range(WW):
            start = KEYS * (WW - 1 - wq)
            piece = turned[:, start : start + WIN]
            row = wq * KEYS + half * WZ * HALF
            for h in range(HEADS):
                bias[h, row : row + WZ * HALF, :] = piece[8 * h : 8 * h + WZ * HALF, :]


def attend(q, k, v, bias):
    head_of = lax.broadcasted_iota(jnp.int32, (WIN, C), 1) // DIM
    scale = LOG2E / float(np.sqrt(DIM))
    zero = jnp.zeros((WIN, C), BF)
    stacked = jnp.concatenate([jnp.where(head_of == h, q, zero) for h in range(HEADS)], axis=0)
    scores = dot_t(stacked, k)
    probs, inverse = [], []
    for h in range(HEADS):
        own = scores[WIN * h : WIN * (h + 1)] * scale + bias[h]
        weights = jnp.exp2(own - jnp.max(own, axis=-1, keepdims=True))
        inverse.append(1.0 / jnp.sum(weights, axis=-1, keepdims=True))
        probs.append(weights.astype(BF))
    values = dot(jnp.concatenate(probs, axis=0), v)
    total = values[0:WIN] * inverse[0]
    for h in range(1, HEADS):
        part = values[WIN * h : WIN * (h + 1)] * inverse[h]
        total = jnp.where(head_of == h, part, total)
    return total.astype(BF)


def block(x, gains, wqkv, wproj, wexp, wred, bqkv, brow, bias):
    floats = x.astype(F32)
    normed = norm(floats, gains[0:1, :], gains[1:2, :]).astype(BF)
    q, k, v = (
        (dot_t(normed, wqkv[C * i : C * (i + 1), :]) + bqkv[i : i + 1, :]).astype(BF)
        for i in range(3)
    )
    windows = (slice(at, at + WIN) for at in range(0, x.shape[0], WIN))
    attended = jnp.concatenate([attend(q[rows], k[rows], v[rows], bias) for rows in windows], axis=0)
    middle = (floats + dot_t(attended, wproj[...]) + brow[1:2, 0:C]).astype(BF)
    middle_floats = middle.astype(F32)
    normed_two = norm(middle_floats, gains[2:3, :], gains[3:4, :]).astype(BF)
    total = middle_floats + brow[2:3, 0:C]
    for at in range(0, MLP, 256):
        pre = dot(normed_two, wexp[:, at : at + 256]) + brow[0:1, at : at + 256]
        hidden = (0.5 * pre * (1.0 + lax.erf(pre * float(np.sqrt(0.5))))).astype(BF)
        total = total + dot(hidden, wred[at : at + 256, :])
    return total.astype(BF)


def daily_kernel(own, other, pick, pack, gains, turn, out_0, out_1, bias, *mats):
    assemble(pack, *mats)
    expand_bias((own, other), turn.at[lax.rem(lax.axis_index("lat"), 2)], bias)

    @pl.when(lax.axis_index("section") == 0)
    def _():
        tokens = []
        for t in range(2):
            rows = slice(WIN * t, WIN * (t + 1))
            source = jnp.concatenate([own[rows, 0:C], other[rows, 0:C]], axis=0)
            tokens.append(dot(pick[...], source).astype(BF))
        result = block(jnp.concatenate(tokens, axis=0), gains, *mats, bias)
        for w, (out, side) in enumerate(((out_0, 0), (out_0, C), (out_1, 0), (out_1, C))):
            out[:, side : side + C] = result[WIN * w : WIN * (w + 1)]


def chained_block(received, own, split, gains, bias, mats, hold):
    section = lax.axis_index("section")

    @pl.when(section == 0)
    def _():
        hold[0:WIN, :] = own[:, 0:C]
        hold[WIN : 2 * WIN, :] = own[:, C : 2 * C]

    @pl.when(section == 1)
    def _():
        x = jnp.concatenate([received[:, 0:C], received[:, C : 2 * C]], axis=0)
        hold[...] = block(x, gains, *mats, bias)

    ordered = dot(split[...], hold[...]).astype(BF)
    return ordered[0:WIN], ordered[WIN : 2 * WIN]


def chained_kernel(received, own, split, gains, bias, *rest):
    *mats, out, hold = rest
    out[0], out[1] = chained_block(received, own, split, gains, bias, mats, hold)


def last_kernel(earlier, received, own, split, gains, bias, *rest):
    *mats, out, hold = rest
    core = lax.rem(lax.axis_index("lat"), 2)
    out[core, 0] = earlier[0]
    out[1 - core, 0] = earlier[1]
    mine, theirs = chained_block(received, own, split, gains, bias, mats, hold)
    out[core, 1] = mine
    out[1 - core, 1] = theirs


def place_kernel(both, out, sems):
    core = lax.rem(lax.axis_index("lat"), 2)
    copies = [
        pltpu.make_async_copy(both.at[side, core], out.at[:, pl.ds(24 * side, 24), :], sems.at[side])
        for side in range(2)
    ]
    for copy in copies:
        copy.start()
    for copy in copies:
        copy.wait()


def call(kernel, out_shape, args, scratch=(), flops=0):
    many = isinstance(out_shape, tuple)
    return pl.pallas_call(
        kernel,
        out_shape=out_shape,
        in_specs=[VMEM] * len(args),
        out_specs=(VMEM,) * len(out_shape) if many else VMEM,
        scratch_shapes=list(scratch),
        compiler_params=PARAMS,
        cost_estimate=pl.CostEstimate(flops=flops, bytes_accessed=1 << 20, transcendentals=0),
    )(*args)


def on_device(
    initial_field,
    first_gain,
    first_shift,
    qkv_weight,
    qkv_bias,
    proj_weight,
    proj_bias,
    second_gain,
    second_shift,
    expand_weight,
    expand_bias_row,
    reduce_weight,
    reduce_bias,
    earth_bias,
):
    lat_count = lax.axis_size("lat")
    pairs = [[2 * i, 2 * i + 1] for i in range(lat_count // 2)]
    shape = jax.ShapeDtypeStruct
    hbm = pl.BlockSpec(memory_space=pltpu.HBM)
    operands = (
        jnp.swapaxes(qkv_weight, 1, 2),
        jnp.swapaxes(proj_weight, 1, 2),
        expand_weight,
        reduce_weight,
        qkv_bias,
        proj_bias,
        expand_bias_row,
        reduce_bias,
        initial_field.reshape(12, 48, C),
        earth_bias.reshape(HEADS, 1, -1),
        first_gain,
        first_shift,
        second_gain,
        second_shift,
    )
    pick = jnp.asarray(pick_rows())
    split = jnp.asarray(pick_rows().T)
    turn = jnp.asarray(turn_columns())
    weights, kept, sent, gains = pl.pallas_call(
        load_kernel,
        out_shape=(
            shape((304, 384), BF),
            shape((576, 256), BF),
            shape((576, 256), BF),
            shape((4, C), F32),
        ),
        in_specs=[hbm] * len(operands),
        out_specs=(VMEM,) * 4,
        scratch_shapes=[
            pltpu.VMEM((144, C), BF),
            pltpu.VMEM((48, C), BF),
            pltpu.VMEM((C, C), BF),
            pltpu.VMEM((C, C), BF),
            pltpu.VMEM((1, 144), BF),
            pltpu.VMEM((1, 48), BF),
            pltpu.VMEM((1, C), BF),
            pltpu.VMEM((1, 48), BF),
            pltpu.VMEM((12, 24, C), BF),
            pltpu.VMEM((12, 24, C), BF),
            pltpu.VMEM((8, 1656), F32),
            pltpu.VMEM((4, 1, C), BF),
            pltpu.VMEM((4, 48, 128), F32),
            pltpu.SemaphoreType.DMA((20,)),
        ],
        compiler_params=PARAMS,
    )(*(pltpu.with_memory_space_constraint(x, pltpu.HBM) for x in operands))
    swap = [(i, i ^ 1) for i in range(lat_count)]
    other = lax.ppermute(sent, "lat", swap)
    shares = lax.all_gather(weights.reshape(2, 152, 2 * C), "tp", axis=0, tiled=True)
    pack = shares.reshape(4, 304, 2 * C)
    mats = (
        shape((3 * C, C), BF),
        shape((C, C), BF),
        shape((C, MLP), BF),
        shape((MLP, C), BF),
        shape((3, C), F32),
        shape((3, MLP), F32),
    )
    flops = 2 * 576 * 192 * 192 * 14
    dense = shape((WIN, 2 * C), BF)
    daily_0, daily_1, bias, *mats = call(
        daily_kernel,
        (dense, dense, shape((HEADS, WIN, WIN), F32), *mats),
        (kept, other, pick, pack, gains, turn),
        flops=flops,
    )
    received_0 = lax.ppermute(daily_0, "section", [(0, 1)])
    received_1 = lax.ppermute(daily_1, "section", [(0, 1)])
    hold = [pltpu.VMEM((2 * WIN, C), BF)]
    shared = (split, gains, bias, *mats)
    earlier = call(
        chained_kernel,
        shape((2, WIN, C), BF),
        (received_0, daily_0, *shared),
        hold,
        flops // 2,
    )
    states = call(
        last_kernel,
        shape((2, 2, WIN, C), BF),
        (earlier, received_1, daily_1, *shared),
        hold,
        flops // 2,
    )
    both = lax.all_gather(states, "lat", axis_index_groups=pairs)
    placed = pl.pallas_call(
        place_kernel,
        out_shape=shape((12, 48, C), BF),
        in_specs=[pl.BlockSpec(memory_space=pl.ANY)],
        out_specs=pl.BlockSpec(memory_space=pl.ANY),
        scratch_shapes=[pltpu.SemaphoreType.DMA((2,))],
        compiler_params=PARAMS,
    )(both.reshape(2, 2, 12, 24, C))
    return placed.reshape(1, 2, 2, 3, 48, C)


def solution(mesh):
    return jax.shard_map(
        on_device,
        mesh=mesh,
        in_specs=(
            P(None, "tp", "lat", None, None),
            P("section", None),
            P("section", None),
            P("section", None, "tp"),
            P("section", "tp"),
            P("section", None, "tp"),
            P("section", "tp"),
            P("section", None),
            P("section", None),
            P("section", None, "tp"),
            P("section", "tp"),
            P("section", "tp", None),
            P("section", "tp"),
            P("section", "tp", "lat", None, None),
        ),
        out_specs=P("section", None, "tp", "lat", None, None),
        check_vma=False,
    )
```

```python
import jax
import jax.numpy as jnp
import numpy as np
from jax import lax
from jax.experimental import pallas as pl
from jax.experimental.pallas import tpu as pltpu
from jax.sharding import PartitionSpec as P

WZ = 2
WH = 6
WW = 12
HALF = WH // 2
C = 192
HEADS = 6
DIM = C // HEADS
WIN = WZ * WH * WW
SPAN = 2 * WW - 1
KEYS = WZ * WH
LINE = KEYS * SPAN
MLP = 768
EPS = 1e-05
LOG2E = 1.4426950408889634
BF = jnp.bfloat16
F32 = jnp.float32
SIDE = WH * SPAN

VMEM = pl.BlockSpec(memory_space=pltpu.VMEM)
PARAMS = pltpu.CompilerParams(vmem_limit_bytes=20 * 1024 * 1024)


def places():
    row = 0
    for w in range(2):
        for wl in range(WW):
            for other in range(2):
                for z in range(WZ):
                    for h in range(HALF):
                        yield row, other, z, h, w * WW + wl
                        row += 1


def pick_rows():
    out = np.zeros((2 * WIN, 2 * WIN), np.float32)
    for row, other, z, h, lon in places():
        out[row, ((other * WZ + z) * HALF + h) * 24 + lon] = 1.0
    return out.astype(BF)


def turn_columns():
    out = np.zeros((2, LINE, LINE), np.float32)
    for core in range(2):
        for zk in range(WZ):
            for hk in range(WH):
                key = ((core ^ (hk // HALF)) * WZ + zk) * HALF + hk % HALF
                for j in range(SPAN):
                    out[core, (zk * WH + hk) * SPAN + j, (SPAN - 1 - j) * KEYS + key] = 1.0
    return out.astype(BF)


def load_kernel(
    qkv,
    proj,
    expand,
    reduce,
    qkv_b,
    proj_b,
    expand_b,
    reduce_b,
    field,
    table,
    g1,
    s1,
    g2,
    s2,
    share,
    kept,
    sent,
    gains_out,
    qkv_v,
    proj_v,
    expand_v,
    reduce_v,
    qkv_bv,
    proj_bv,
    expand_bv,
    reduce_bv,
    kept_v,
    sent_v,
    table_v,
    gains_v,
    lines,
    weights,
    sems,
):
    core = lax.rem(lax.axis_index("lat"), 2)
    moves = [(table.at[h], table_v.at[pl.ds(h, 1), :]) for h in range(HEADS)]
    moves += [
        (field.at[:, pl.ds(pl.multiple_of(24 * core, 8), 24), :], kept_v),
        (field.at[:, pl.ds(pl.multiple_of(24 - 24 * core, 8), 24), :], sent_v),
        (expand.at[0], expand_v),
        (reduce.at[0], reduce_v),
        (qkv.at[0], qkv_v),
        (proj.at[0], proj_v),
        (qkv_b, qkv_bv),
        (proj_b, proj_bv),
        (expand_b, expand_bv),
        (reduce_b, reduce_bv),
    ]
    moves += [(ref, gains_v.at[i]) for i, ref in enumerate((g1, s1, g2, s2))]
    copies = [pltpu.make_async_copy(a, b, sems.at[i]) for i, (a, b) in enumerate(moves)]
    for copy in copies:
        copy.start()
    weights[288:304, :] = jnp.zeros((16, 384), BF)
    lines[...] = jnp.zeros_like(lines)
    blank = jnp.zeros((HEADS, 256 - SIDE), F32)
    for copy in copies[:HEADS]:
        copy.wait()
    for zr in range(WZ * HALF):
        z, r = divmod(zr, HALF)
        for zk in range(WZ):
            start = ((z * WZ + zk) * HALF + r) * SIDE
            target = pl.ds(zr, HEADS, stride=8)
            lines[2 * zk, target, :] = table_v[0:HEADS, start : start + 128]
            tail = table_v[0:HEADS, start + 128 : start + SIDE]
            lines[2 * zk + 1, target, :] = jnp.concatenate([tail, blank], axis=1)
    for zk in range(WZ):
        whole = jnp.concatenate([lines[2 * zk], lines[2 * zk + 1]], axis=1)
        high = whole.astype(BF)
        rest = whole - high.astype(F32)
        middle = rest.astype(BF)
        low = (rest - middle.astype(F32)).astype(BF)
        for i, part in enumerate((high, middle, low)):
            rows = slice(288 + 144 * zk + 48 * i, 288 + 144 * zk + 48 * (i + 1))
            kept[rows, :] = part
            sent[rows, :] = part
    arrived = iter(copies[HEADS:])
    next(arrived).wait()
    kept[0:288, 0:C] = kept_v[...].reshape(288, C)
    next(arrived).wait()
    sent[0:288, 0:C] = sent_v[...].reshape(288, C)
    next(arrived).wait()
    weights[0:192, 192:384] = expand_v[...]
    next(arrived).wait()
    weights[192:288, 0:192] = reduce_v[0:96, :]
    weights[192:288, 192:384] = reduce_v[96:192, :]
    next(arrived).wait()
    weights[0:144, 0:192] = qkv_v[...]
    next(arrived).wait()
    weights[144:192, 0:192] = proj_v[...]
    for copy in arrived:
        copy.wait()
    weights[288:289, 0:144] = qkv_bv[...]
    weights[288:289, 144:192] = proj_bv[...]
    weights[288:289, 192:384] = expand_bv[...]
    weights[289:290, 0:48] = reduce_bv[...]
    for i in range(4):
        gains_out[i : i + 1, :] = gains_v[i].astype(F32)
    share[...] = weights[pl.ds(pl.multiple_of(144 * core, 16), 160), :]


def join_kernel(own, first, second, third, out):
    me = lax.axis_index("tp")
    out[me] = own[...]
    for k, ref in ((1, first), (3, second), (2, third)):
        out[me ^ k] = ref[...]


def norm(x, gain, shift):
    mean = jnp.sum(x, axis=-1, keepdims=True) * (1.0 / C)
    centred = x - mean
    var = jnp.sum(centred * centred, axis=-1, keepdims=True) * (1.0 / C)
    return centred * lax.rsqrt(var + EPS) * gain + shift


def dot(a, b):
    return jnp.dot(a, b, preferred_element_type=F32)


def dot_t(a, b):
    return lax.dot_general(a, b, (((1,), (1,)), ((), ())), preferred_element_type=F32)


def assemble(pack, wqkv, wproj, wexp, wred, bqkv, brow):
    for j in range(4):
        low, high = pack.at[0, j], pack.at[1, j]
        wqkv[144 * j : 144 * (j + 1), :] = low[0:144, 0:C]
        wproj[48 * j : 48 * (j + 1), :] = high[0:48, 0:C]
        wexp[0:144, C * j : C * (j + 1)] = low[0:144, C : 2 * C]
        wexp[144:192, C * j : C * (j + 1)] = high[0:48, C : 2 * C]
        wred[C * j : C * j + 96, :] = high[48:144, 0:C]
        wred[C * j + 96 : C * (j + 1), :] = high[48:144, C : 2 * C]
        brow[0:1, C * j : C * (j + 1)] = high[144:145, C : 2 * C].astype(F32)
        brow[1:2, 48 * j : 48 * (j + 1)] = high[144:145, 144:192].astype(F32)
        brow[2:3, 48 * j : 48 * (j + 1)] = high[145:146, 0:48].astype(F32)
        at = 144 * j
        while at < 144 * (j + 1):
            part, inner = divmod(at, C)
            size = min(C - inner, 144 * (j + 1) - at)
            source = at - 144 * j
            bqkv[part : part + 1, inner : inner + size] = high[
                144:145, source : source + size
            ].astype(F32)
            at += size


def expand_bias(fields, turn, bias):
    for half, field in enumerate(fields):
        parts = None
        for zk in range(WZ):
            rows = slice(288 + 144 * zk, 288 + 144 * (zk + 1))
            part = dot(field[rows, 0:SIDE], turn[SIDE * zk : SIDE * (zk + 1), :])
            parts = part if parts is None else parts + part
        turned = (parts[0:48] + parts[48:96] + parts[96:144]) * LOG2E
        for wq in range(WW):
            start = KEYS * (WW - 1 - wq)
            piece = turned[:, start : start + WIN]
            row = wq * KEYS + half * WZ * HALF
            for h in range(HEADS):
                bias[h, row : row + WZ * HALF, :] = piece[8 * h : 8 * h + WZ * HALF, :]


def attend(q, k, v, bias):
    head_of = lax.broadcasted_iota(jnp.int32, (WIN, C), 1) // DIM
    scale = LOG2E / float(np.sqrt(DIM))
    zero = jnp.zeros((WIN, C), BF)
    stacked = jnp.concatenate([jnp.where(head_of == h, q, zero) for h in range(HEADS)], axis=0)
    scores = dot_t(stacked, k)
    probs, inverse = [], []
    for h in range(HEADS):
        own = scores[WIN * h : WIN * (h + 1)] * scale + bias[h]
        weights = jnp.exp2(own - jnp.max(own, axis=-1, keepdims=True))
        inverse.append(1.0 / jnp.sum(weights, axis=-1, keepdims=True))
        probs.append(weights.astype(BF))
    values = dot(jnp.concatenate(probs, axis=0), v)
    total = values[0:WIN] * inverse[0]
    for h in range(1, HEADS):
        part = values[WIN * h : WIN * (h + 1)] * inverse[h]
        total = jnp.where(head_of == h, part, total)
    return total.astype(BF)


def block(x, gains, wqkv, wproj, wexp, wred, bqkv, brow, bias):
    floats = x.astype(F32)
    normed = norm(floats, gains[0:1, :], gains[1:2, :]).astype(BF)
    q, k, v = (
        (dot_t(normed, wqkv[C * i : C * (i + 1), :]) + bqkv[i : i + 1, :]).astype(BF)
        for i in range(3)
    )
    windows = (slice(at, at + WIN) for at in range(0, x.shape[0], WIN))
    attended = jnp.concatenate([attend(q[rows], k[rows], v[rows], bias) for rows in windows], axis=0)
    middle = (floats + dot_t(attended, wproj[...]) + brow[1:2, 0:C]).astype(BF)
    middle_floats = middle.astype(F32)
    normed_two = norm(middle_floats, gains[2:3, :], gains[3:4, :]).astype(BF)
    total = middle_floats + brow[2:3, 0:C]
    for at in range(0, MLP, 256):
        pre = dot(normed_two, wexp[:, at : at + 256]) + brow[0:1, at : at + 256]
        hidden = (0.5 * pre * (1.0 + lax.erf(pre * float(np.sqrt(0.5))))).astype(BF)
        total = total + dot(hidden, wred[at : at + 256, :])
    return total.astype(BF)


def daily_kernel(own, other, pick, pack, gains, turn, out_0, out_1, bias, *mats):
    assemble(pack, *mats)
    expand_bias((own, other), turn.at[lax.rem(lax.axis_index("lat"), 2)], bias)

    @pl.when(lax.axis_index("section") == 0)
    def _():
        tokens = []
        for t in range(2):
            rows = slice(WIN * t, WIN * (t + 1))
            source = jnp.concatenate([own[rows, 0:C], other[rows, 0:C]], axis=0)
            tokens.append(dot(pick[...], source).astype(BF))
        result = block(jnp.concatenate(tokens, axis=0), gains, *mats, bias)
        for w, (out, side) in enumerate(((out_0, 0), (out_0, C), (out_1, 0), (out_1, C))):
            out[:, side : side + C] = result[WIN * w : WIN * (w + 1)]


def chained_block(received, own, split, gains, bias, mats, hold):
    section = lax.axis_index("section")

    @pl.when(section == 0)
    def _():
        hold[0:WIN, :] = own[:, 0:C]
        hold[WIN : 2 * WIN, :] = own[:, C : 2 * C]

    @pl.when(section == 1)
    def _():
        x = jnp.concatenate([received[:, 0:C], received[:, C : 2 * C]], axis=0)
        hold[...] = block(x, gains, *mats, bias)

    ordered = dot(split[...], hold[...]).astype(BF)
    return ordered[0:WIN], ordered[WIN : 2 * WIN]


def chained_kernel(received, own, split, gains, bias, *rest):
    *mats, out, hold = rest
    out[0], out[1] = chained_block(received, own, split, gains, bias, mats, hold)


def last_kernel(earlier, received, own, split, gains, bias, *rest):
    *mats, out, hold = rest
    core = lax.rem(lax.axis_index("lat"), 2)
    out[core, 0] = earlier[0]
    out[1 - core, 0] = earlier[1]
    mine, theirs = chained_block(received, own, split, gains, bias, mats, hold)
    out[core, 1] = mine
    out[1 - core, 1] = theirs


def place_kernel(both, out, sems):
    core = lax.rem(lax.axis_index("lat"), 2)
    copies = [
        pltpu.make_async_copy(both.at[side, core], out.at[:, pl.ds(24 * side, 24), :], sems.at[side])
        for side in range(2)
    ]
    for copy in copies:
        copy.start()
    for copy in copies:
        copy.wait()


def call(kernel, out_shape, args, scratch=(), flops=0):
    many = isinstance(out_shape, tuple)
    return pl.pallas_call(
        kernel,
        out_shape=out_shape,
        in_specs=[VMEM] * len(args),
        out_specs=(VMEM,) * len(out_shape) if many else VMEM,
        scratch_shapes=list(scratch),
        compiler_params=PARAMS,
        cost_estimate=pl.CostEstimate(flops=flops, bytes_accessed=1 << 20, transcendentals=0),
    )(*args)


def on_device(
    initial_field,
    first_gain,
    first_shift,
    qkv_weight,
    qkv_bias,
    proj_weight,
    proj_bias,
    second_gain,
    second_shift,
    expand_weight,
    expand_bias_row,
    reduce_weight,
    reduce_bias,
    earth_bias,
):
    lat_count = lax.axis_size("lat")
    pairs = [[2 * i, 2 * i + 1] for i in range(lat_count // 2)]
    shape = jax.ShapeDtypeStruct
    hbm = pl.BlockSpec(memory_space=pltpu.HBM)
    operands = (
        jnp.swapaxes(qkv_weight, 1, 2),
        jnp.swapaxes(proj_weight, 1, 2),
        expand_weight,
        reduce_weight,
        qkv_bias,
        proj_bias,
        expand_bias_row,
        reduce_bias,
        initial_field.reshape(12, 48, C),
        earth_bias.reshape(HEADS, 1, -1),
        first_gain,
        first_shift,
        second_gain,
        second_shift,
    )
    pick = jnp.asarray(pick_rows())
    split = jnp.asarray(pick_rows().T)
    turn = jnp.asarray(turn_columns())
    share, kept, sent, gains = pl.pallas_call(
        load_kernel,
        out_shape=(
            shape((160, 2 * C), BF),
            shape((576, 256), BF),
            shape((576, 256), BF),
            shape((4, C), F32),
        ),
        in_specs=[hbm] * len(operands),
        out_specs=(VMEM,) * 4,
        scratch_shapes=[
            pltpu.VMEM((144, C), BF),
            pltpu.VMEM((48, C), BF),
            pltpu.VMEM((C, C), BF),
            pltpu.VMEM((C, C), BF),
            pltpu.VMEM((1, 144), BF),
            pltpu.VMEM((1, 48), BF),
            pltpu.VMEM((1, C), BF),
            pltpu.VMEM((1, 48), BF),
            pltpu.VMEM((12, 24, C), BF),
            pltpu.VMEM((12, 24, C), BF),
            pltpu.VMEM((8, 1656), F32),
            pltpu.VMEM((4, 1, C), BF),
            pltpu.VMEM((4, 48, 128), F32),
            pltpu.VMEM((304, 2 * C), BF),
            pltpu.SemaphoreType.DMA((20,)),
        ],
        compiler_params=PARAMS,
    )(*(pltpu.with_memory_space_constraint(x, pltpu.HBM) for x in operands))
    shares = [
        lax.ppermute(share, "tp", [(i, i ^ k) for i in range(lax.axis_size("tp"))]) for k in (1, 3, 2)
    ]
    swap = [(i, i ^ 1) for i in range(lat_count)]
    other = lax.ppermute(sent, "lat", swap)
    joined = call(join_kernel, shape((4, 160, 2 * C), BF), (share, *shares))
    pack = lax.all_gather(joined, "lat", axis_index_groups=pairs)
    mats = (
        shape((3 * C, C), BF),
        shape((C, C), BF),
        shape((C, MLP), BF),
        shape((MLP, C), BF),
        shape((3, C), F32),
        shape((3, MLP), F32),
    )
    flops = 2 * 576 * 192 * 192 * 14
    dense = shape((WIN, 2 * C), BF)
    daily_0, daily_1, bias, *mats = call(
        daily_kernel,
        (dense, dense, shape((HEADS, WIN, WIN), F32), *mats),
        (kept, other, pick, pack, gains, turn),
        flops=flops,
    )
    received_0 = lax.ppermute(daily_0, "section", [(0, 1)])
    received_1 = lax.ppermute(daily_1, "section", [(0, 1)])
    hold = [pltpu.VMEM((2 * WIN, C), BF)]
    shared = (split, gains, bias, *mats)
    earlier = call(
        chained_kernel,
        shape((2, WIN, C), BF),
        (received_0, daily_0, *shared),
        hold,
        flops // 2,
    )
    states = call(
        last_kernel,
        shape((2, 2, WIN, C), BF),
        (earlier, received_1, daily_1, *shared),
        hold,
        flops // 2,
    )
    both = lax.all_gather(states, "lat", axis_index_groups=pairs)
    placed = pl.pallas_call(
        place_kernel,
        out_shape=shape((12, 48, C), BF),
        in_specs=[pl.BlockSpec(memory_space=pl.ANY)],
        out_specs=pl.BlockSpec(memory_space=pl.ANY),
        scratch_shapes=[pltpu.SemaphoreType.DMA((2,))],
        compiler_params=PARAMS,
    )(both.reshape(2, 2, 12, 24, C))
    return placed.reshape(1, 2, 2, 3, 48, C)


def solution(mesh):
    return jax.shard_map(
        on_device,
        mesh=mesh,
        in_specs=(
            P(None, "tp", "lat", None, None),
            P("section", None),
            P("section", None),
            P("section", None, "tp"),
            P("section", "tp"),
            P("section", None, "tp"),
            P("section", "tp"),
            P("section", None),
            P("section", None),
            P("section", None, "tp"),
            P("section", "tp"),
            P("section", "tp", None),
            P("section", "tp"),
            P("section", "tp", "lat", None, None),
        ),
        out_specs=P("section", None, "tp", "lat", None, None),
        check_vma=False,
    )
```

```python
import jax
import jax.numpy as jnp
import numpy as np
from jax import lax
from jax.experimental import pallas as pl
from jax.experimental.pallas import tpu as pltpu
from jax.sharding import PartitionSpec as P

WZ = 2
WH = 6
WW = 12
HALF = WH // 2
C = 192
HEADS = 6
DIM = C // HEADS
WIN = WZ * WH * WW
SPAN = 2 * WW - 1
KEYS = WZ * WH
LINE = KEYS * SPAN
MLP = 768
EPS = 1e-05
LOG2E = 1.4426950408889634
BF = jnp.bfloat16
F32 = jnp.float32
SIDE = WH * SPAN

VMEM = pl.BlockSpec(memory_space=pltpu.VMEM)
PARAMS = pltpu.CompilerParams(vmem_limit_bytes=20 * 1024 * 1024)


def places():
    row = 0
    for w in range(2):
        for wl in range(WW):
            for other in range(2):
                for z in range(WZ):
                    for h in range(HALF):
                        yield row, other, z, h, w * WW + wl
                        row += 1


def pick_rows():
    out = np.zeros((2 * WIN, 2 * WIN), np.float32)
    for row, other, z, h, lon in places():
        out[row, ((other * WZ + z) * HALF + h) * 24 + lon] = 1.0
    return out.astype(BF)


def turn_columns():
    out = np.zeros((2, LINE, LINE), np.float32)
    for core in range(2):
        for zk in range(WZ):
            for hk in range(WH):
                key = ((core ^ (hk // HALF)) * WZ + zk) * HALF + hk % HALF
                for j in range(SPAN):
                    out[core, (zk * WH + hk) * SPAN + j, (SPAN - 1 - j) * KEYS + key] = 1.0
    return out.astype(BF)


def load_kernel(
    qkv,
    proj,
    expand,
    reduce,
    qkv_b,
    proj_b,
    expand_b,
    reduce_b,
    field,
    table,
    g1,
    s1,
    g2,
    s2,
    share,
    kept,
    sent,
    gains_out,
    qkv_v,
    proj_v,
    expand_v,
    reduce_v,
    qkv_bv,
    proj_bv,
    expand_bv,
    reduce_bv,
    kept_v,
    sent_v,
    table_v,
    gains_v,
    lines,
    weights,
    sems,
):
    core = lax.rem(lax.axis_index("lat"), 2)
    moves = [(table.at[h], table_v.at[pl.ds(h, 1), :]) for h in range(HEADS)]
    moves += [
        (field.at[:, pl.ds(pl.multiple_of(24 * core, 8), 24), :], kept_v),
        (field.at[:, pl.ds(pl.multiple_of(24 - 24 * core, 8), 24), :], sent_v),
        (expand.at[0], expand_v),
        (reduce.at[0], reduce_v),
        (qkv.at[0], qkv_v),
        (proj.at[0], proj_v),
        (qkv_b, qkv_bv),
        (proj_b, proj_bv),
        (expand_b, expand_bv),
        (reduce_b, reduce_bv),
    ]
    moves += [(ref, gains_v.at[i]) for i, ref in enumerate((g1, s1, g2, s2))]
    copies = [pltpu.make_async_copy(a, b, sems.at[i]) for i, (a, b) in enumerate(moves)]
    for copy in copies:
        copy.start()
    weights[288:304, :] = jnp.zeros((16, 384), BF)
    lines[...] = jnp.zeros_like(lines)
    blank = jnp.zeros((HEADS, 256 - SIDE), F32)
    for copy in copies[:HEADS]:
        copy.wait()
    for zr in range(WZ * HALF):
        z, r = divmod(zr, HALF)
        for zk in range(WZ):
            start = ((z * WZ + zk) * HALF + r) * SIDE
            target = pl.ds(zr, HEADS, stride=8)
            lines[2 * zk, target, :] = table_v[0:HEADS, start : start + 128]
            tail = table_v[0:HEADS, start + 128 : start + SIDE]
            lines[2 * zk + 1, target, :] = jnp.concatenate([tail, blank], axis=1)
    for zk in range(WZ):
        whole = jnp.concatenate([lines[2 * zk], lines[2 * zk + 1]], axis=1)
        high = whole.astype(BF)
        rest = whole - high.astype(F32)
        middle = rest.astype(BF)
        low = (rest - middle.astype(F32)).astype(BF)
        for i, part in enumerate((high, middle, low)):
            rows = slice(288 + 144 * zk + 48 * i, 288 + 144 * zk + 48 * (i + 1))
            kept[rows, :] = part
            sent[rows, :] = part
    arrived = iter(copies[HEADS:])
    next(arrived).wait()
    kept[0:288, 0:C] = kept_v[...].reshape(288, C)
    next(arrived).wait()
    sent[0:288, 0:C] = sent_v[...].reshape(288, C)
    next(arrived).wait()
    weights[0:192, 192:384] = expand_v[...]
    next(arrived).wait()
    weights[192:288, 0:192] = reduce_v[0:96, :]
    weights[192:288, 192:384] = reduce_v[96:192, :]
    next(arrived).wait()
    weights[0:144, 0:192] = qkv_v[...]
    next(arrived).wait()
    weights[144:192, 0:192] = proj_v[...]
    for copy in arrived:
        copy.wait()
    weights[288:289, 0:144] = qkv_bv[...]
    weights[288:289, 144:192] = proj_bv[...]
    weights[288:289, 192:384] = expand_bv[...]
    weights[289:290, 0:48] = reduce_bv[...]
    for i in range(4):
        gains_out[i : i + 1, :] = gains_v[i].astype(F32)
    share[...] = weights[pl.ds(pl.multiple_of(144 * core, 16), 160), :]


def join_kernel(own, first, second, third, out):
    me = lax.axis_index("tp")
    out[me] = own[...]
    for k, ref in ((3, first), (1, second), (2, third)):
        out[lax.rem(me + 4 - k, 4)] = ref[...]


def norm(x, gain, shift):
    mean = jnp.sum(x, axis=-1, keepdims=True) * (1.0 / C)
    centred = x - mean
    var = jnp.sum(centred * centred, axis=-1, keepdims=True) * (1.0 / C)
    return centred * lax.rsqrt(var + EPS) * gain + shift


def dot(a, b):
    return jnp.dot(a, b, preferred_element_type=F32)


def dot_t(a, b):
    return lax.dot_general(a, b, (((1,), (1,)), ((), ())), preferred_element_type=F32)


def assemble(pack, wqkv, wproj, wexp, wred, bqkv, brow):
    for j in range(4):
        low, high = pack.at[0, j], pack.at[1, j]
        wqkv[144 * j : 144 * (j + 1), :] = low[0:144, 0:C]
        wproj[48 * j : 48 * (j + 1), :] = high[0:48, 0:C]
        wexp[0:144, C * j : C * (j + 1)] = low[0:144, C : 2 * C]
        wexp[144:192, C * j : C * (j + 1)] = high[0:48, C : 2 * C]
        wred[C * j : C * j + 96, :] = high[48:144, 0:C]
        wred[C * j + 96 : C * (j + 1), :] = high[48:144, C : 2 * C]
        brow[0:1, C * j : C * (j + 1)] = high[144:145, C : 2 * C].astype(F32)
        brow[1:2, 48 * j : 48 * (j + 1)] = high[144:145, 144:192].astype(F32)
        brow[2:3, 48 * j : 48 * (j + 1)] = high[145:146, 0:48].astype(F32)
        at = 144 * j
        while at < 144 * (j + 1):
            part, inner = divmod(at, C)
            size = min(C - inner, 144 * (j + 1) - at)
            source = at - 144 * j
            bqkv[part : part + 1, inner : inner + size] = high[
                144:145, source : source + size
            ].astype(F32)
            at += size


def expand_bias(fields, turn, bias):
    for half, field in enumerate(fields):
        parts = None
        for zk in range(WZ):
            rows = slice(288 + 144 * zk, 288 + 144 * (zk + 1))
            part = dot(field[rows, 0:SIDE], turn[SIDE * zk : SIDE * (zk + 1), :])
            parts = part if parts is None else parts + part
        turned = (parts[0:48] + parts[48:96] + parts[96:144]) * LOG2E
        for wq in range(WW):
            start = KEYS * (WW - 1 - wq)
            piece = turned[:, start : start + WIN]
            row = wq * KEYS + half * WZ * HALF
            for h in range(HEADS):
                bias[h, row : row + WZ * HALF, :] = piece[8 * h : 8 * h + WZ * HALF, :]


def attend(q, k, v, bias):
    head_of = lax.broadcasted_iota(jnp.int32, (WIN, C), 1) // DIM
    scale = LOG2E / float(np.sqrt(DIM))
    zero = jnp.zeros((WIN, C), BF)
    stacked = jnp.concatenate([jnp.where(head_of == h, q, zero) for h in range(HEADS)], axis=0)
    scores = dot_t(stacked, k)
    probs, inverse = [], []
    for h in range(HEADS):
        own = scores[WIN * h : WIN * (h + 1)] * scale + bias[h]
        weights = jnp.exp2(own - jnp.max(own, axis=-1, keepdims=True))
        inverse.append(1.0 / jnp.sum(weights, axis=-1, keepdims=True))
        probs.append(weights.astype(BF))
    values = dot(jnp.concatenate(probs, axis=0), v)
    total = values[0:WIN] * inverse[0]
    for h in range(1, HEADS):
        part = values[WIN * h : WIN * (h + 1)] * inverse[h]
        total = jnp.where(head_of == h, part, total)
    return total.astype(BF)


def block(x, gains, wqkv, wproj, wexp, wred, bqkv, brow, bias):
    floats = x.astype(F32)
    normed = norm(floats, gains[0:1, :], gains[1:2, :]).astype(BF)
    q, k, v = (
        (dot_t(normed, wqkv[C * i : C * (i + 1), :]) + bqkv[i : i + 1, :]).astype(BF)
        for i in range(3)
    )
    windows = (slice(at, at + WIN) for at in range(0, x.shape[0], WIN))
    attended = jnp.concatenate([attend(q[rows], k[rows], v[rows], bias) for rows in windows], axis=0)
    middle = (floats + dot_t(attended, wproj[...]) + brow[1:2, 0:C]).astype(BF)
    middle_floats = middle.astype(F32)
    normed_two = norm(middle_floats, gains[2:3, :], gains[3:4, :]).astype(BF)
    total = middle_floats + brow[2:3, 0:C]
    for at in range(0, MLP, 256):
        pre = dot(normed_two, wexp[:, at : at + 256]) + brow[0:1, at : at + 256]
        hidden = (0.5 * pre * (1.0 + lax.erf(pre * float(np.sqrt(0.5))))).astype(BF)
        total = total + dot(hidden, wred[at : at + 256, :])
    return total.astype(BF)


def daily_kernel(own, other, pick, pack, gains, turn, out_0, out_1, bias, *mats):
    assemble(pack, *mats)
    expand_bias((own, other), turn.at[lax.rem(lax.axis_index("lat"), 2)], bias)

    @pl.when(lax.axis_index("section") == 0)
    def _():
        tokens = []
        for t in range(2):
            rows = slice(WIN * t, WIN * (t + 1))
            source = jnp.concatenate([own[rows, 0:C], other[rows, 0:C]], axis=0)
            tokens.append(dot(pick[...], source).astype(BF))
        result = block(jnp.concatenate(tokens, axis=0), gains, *mats, bias)
        for w, (out, side) in enumerate(((out_0, 0), (out_0, C), (out_1, 0), (out_1, C))):
            out[:, side : side + C] = result[WIN * w : WIN * (w + 1)]


def chained_block(received, own, split, gains, bias, mats, hold):
    section = lax.axis_index("section")

    @pl.when(section == 0)
    def _():
        hold[0:WIN, :] = own[:, 0:C]
        hold[WIN : 2 * WIN, :] = own[:, C : 2 * C]

    @pl.when(section == 1)
    def _():
        x = jnp.concatenate([received[:, 0:C], received[:, C : 2 * C]], axis=0)
        hold[...] = block(x, gains, *mats, bias)

    ordered = dot(split[...], hold[...]).astype(BF)
    return ordered[0:WIN], ordered[WIN : 2 * WIN]


def chained_kernel(received, own, split, gains, bias, *rest):
    *mats, out, hold = rest
    out[0], out[1] = chained_block(received, own, split, gains, bias, mats, hold)


def last_kernel(earlier, received, own, split, gains, bias, *rest):
    *mats, out, hold = rest
    core = lax.rem(lax.axis_index("lat"), 2)
    out[core, 0] = earlier[0]
    out[1 - core, 0] = earlier[1]
    mine, theirs = chained_block(received, own, split, gains, bias, mats, hold)
    out[core, 1] = mine
    out[1 - core, 1] = theirs


def place_kernel(both, out, sems):
    core = lax.rem(lax.axis_index("lat"), 2)
    copies = [
        pltpu.make_async_copy(both.at[side, core], out.at[:, pl.ds(24 * side, 24), :], sems.at[side])
        for side in range(2)
    ]
    for copy in copies:
        copy.start()
    for copy in copies:
        copy.wait()


def call(kernel, out_shape, args, scratch=(), flops=0):
    many = isinstance(out_shape, tuple)
    return pl.pallas_call(
        kernel,
        out_shape=out_shape,
        in_specs=[VMEM] * len(args),
        out_specs=(VMEM,) * len(out_shape) if many else VMEM,
        scratch_shapes=list(scratch),
        compiler_params=PARAMS,
        cost_estimate=pl.CostEstimate(flops=flops, bytes_accessed=1 << 20, transcendentals=0),
    )(*args)


def on_device(
    initial_field,
    first_gain,
    first_shift,
    qkv_weight,
    qkv_bias,
    proj_weight,
    proj_bias,
    second_gain,
    second_shift,
    expand_weight,
    expand_bias_row,
    reduce_weight,
    reduce_bias,
    earth_bias,
):
    lat_count = lax.axis_size("lat")
    pairs = [[2 * i, 2 * i + 1] for i in range(lat_count // 2)]
    shape = jax.ShapeDtypeStruct
    hbm = pl.BlockSpec(memory_space=pltpu.HBM)
    operands = (
        jnp.swapaxes(qkv_weight, 1, 2),
        jnp.swapaxes(proj_weight, 1, 2),
        expand_weight,
        reduce_weight,
        qkv_bias,
        proj_bias,
        expand_bias_row,
        reduce_bias,
        initial_field.reshape(12, 48, C),
        earth_bias.reshape(HEADS, 1, -1),
        first_gain,
        first_shift,
        second_gain,
        second_shift,
    )
    pick = jnp.asarray(pick_rows())
    split = jnp.asarray(pick_rows().T)
    turn = jnp.asarray(turn_columns())
    share, kept, sent, gains = pl.pallas_call(
        load_kernel,
        out_shape=(
            shape((160, 2 * C), BF),
            shape((576, 256), BF),
            shape((576, 256), BF),
            shape((4, C), F32),
        ),
        in_specs=[hbm] * len(operands),
        out_specs=(VMEM,) * 4,
        scratch_shapes=[
            pltpu.VMEM((144, C), BF),
            pltpu.VMEM((48, C), BF),
            pltpu.VMEM((C, C), BF),
            pltpu.VMEM((C, C), BF),
            pltpu.VMEM((1, 144), BF),
            pltpu.VMEM((1, 48), BF),
            pltpu.VMEM((1, C), BF),
            pltpu.VMEM((1, 48), BF),
            pltpu.VMEM((12, 24, C), BF),
            pltpu.VMEM((12, 24, C), BF),
            pltpu.VMEM((8, 1656), F32),
            pltpu.VMEM((4, 1, C), BF),
            pltpu.VMEM((4, 48, 128), F32),
            pltpu.VMEM((304, 2 * C), BF),
            pltpu.SemaphoreType.DMA((20,)),
        ],
        compiler_params=PARAMS,
    )(*(pltpu.with_memory_space_constraint(x, pltpu.HBM) for x in operands))
    tp_count = lax.axis_size("tp")
    shares = [
        lax.ppermute(share, "tp", [(i, (i + k) % tp_count) for i in range(tp_count)]) for k in (3, 1, 2)
    ]
    swap = [(i, i ^ 1) for i in range(lat_count)]
    other = lax.ppermute(sent, "lat", swap)
    joined = call(join_kernel, shape((4, 160, 2 * C), BF), (share, *shares))
    pack = lax.all_gather(joined, "lat", axis_index_groups=pairs)
    mats = (
        shape((3 * C, C), BF),
        shape((C, C), BF),
        shape((C, MLP), BF),
        shape((MLP, C), BF),
        shape((3, C), F32),
        shape((3, MLP), F32),
    )
    flops = 2 * 576 * 192 * 192 * 14
    dense = shape((WIN, 2 * C), BF)
    daily_0, daily_1, bias, *mats = call(
        daily_kernel,
        (dense, dense, shape((HEADS, WIN, WIN), F32), *mats),
        (kept, other, pick, pack, gains, turn),
        flops=flops,
    )
    received_0 = lax.ppermute(daily_0, "section", [(0, 1)])
    received_1 = lax.ppermute(daily_1, "section", [(0, 1)])
    hold = [pltpu.VMEM((2 * WIN, C), BF)]
    shared = (split, gains, bias, *mats)
    earlier = call(
        chained_kernel,
        shape((2, WIN, C), BF),
        (received_0, daily_0, *shared),
        hold,
        flops // 2,
    )
    states = call(
        last_kernel,
        shape((2, 2, WIN, C), BF),
        (earlier, received_1, daily_1, *shared),
        hold,
        flops // 2,
    )
    both = lax.all_gather(states, "lat", axis_index_groups=pairs)
    placed = pl.pallas_call(
        place_kernel,
        out_shape=shape((12, 48, C), BF),
        in_specs=[pl.BlockSpec(memory_space=pl.ANY)],
        out_specs=pl.BlockSpec(memory_space=pl.ANY),
        scratch_shapes=[pltpu.SemaphoreType.DMA((2,))],
        compiler_params=PARAMS,
    )(both.reshape(2, 2, 12, 24, C))
    return placed.reshape(1, 2, 2, 3, 48, C)


def solution(mesh):
    return jax.shard_map(
        on_device,
        mesh=mesh,
        in_specs=(
            P(None, "tp", "lat", None, None),
            P("section", None),
            P("section", None),
            P("section", None, "tp"),
            P("section", "tp"),
            P("section", None, "tp"),
            P("section", "tp"),
            P("section", None),
            P("section", None),
            P("section", None, "tp"),
            P("section", "tp"),
            P("section", "tp", None),
            P("section", "tp"),
            P("section", "tp", "lat", None, None),
        ),
        out_specs=P("section", None, "tp", "lat", None, None),
        check_vma=False,
    )
```

```python
import jax
import jax.numpy as jnp
import numpy as np
from jax import lax
from jax.experimental import pallas as pl
from jax.experimental.pallas import tpu as pltpu
from jax.sharding import PartitionSpec as P

WZ = 2
WH = 6
WW = 12
HALF = WH // 2
C = 192
HEADS = 6
DIM = C // HEADS
WIN = WZ * WH * WW
SPAN = 2 * WW - 1
KEYS = WZ * WH
LINE = KEYS * SPAN
MLP = 768
EPS = 1e-05
LOG2E = 1.4426950408889634
BF = jnp.bfloat16
F32 = jnp.float32
SIDE = WH * SPAN

VMEM = pl.BlockSpec(memory_space=pltpu.VMEM)
PARAMS = pltpu.CompilerParams(vmem_limit_bytes=20 * 1024 * 1024)


def places():
    row = 0
    for w in range(2):
        for wl in range(WW):
            for other in range(2):
                for z in range(WZ):
                    for h in range(HALF):
                        yield row, other, z, h, w * WW + wl
                        row += 1


def pick_rows():
    out = np.zeros((2 * WIN, 2 * WIN), np.float32)
    for row, other, z, h, lon in places():
        out[row, ((other * WZ + z) * HALF + h) * 24 + lon] = 1.0
    return out.astype(BF)


def turn_columns():
    out = np.zeros((2, LINE, LINE), np.float32)
    for core in range(2):
        for zk in range(WZ):
            for hk in range(WH):
                key = ((core ^ (hk // HALF)) * WZ + zk) * HALF + hk % HALF
                for j in range(SPAN):
                    out[core, (zk * WH + hk) * SPAN + j, (SPAN - 1 - j) * KEYS + key] = 1.0
    return out.astype(BF)


def load_kernel(
    qkv,
    proj,
    expand,
    reduce,
    qkv_b,
    proj_b,
    expand_b,
    reduce_b,
    field,
    table,
    g1,
    s1,
    g2,
    s2,
    share,
    kept,
    sent,
    gains_out,
    qkv_v,
    proj_v,
    expand_v,
    reduce_v,
    qkv_bv,
    proj_bv,
    expand_bv,
    reduce_bv,
    kept_v,
    sent_v,
    table_v,
    gains_v,
    lines,
    weights,
    sems,
):
    core = lax.rem(lax.axis_index("lat"), 2)
    moves = [(table.at[h], table_v.at[pl.ds(h, 1), :]) for h in range(HEADS)]
    moves += [
        (field.at[:, pl.ds(pl.multiple_of(24 * core, 8), 24), :], kept_v),
        (field.at[:, pl.ds(pl.multiple_of(24 - 24 * core, 8), 24), :], sent_v),
        (expand.at[0], expand_v),
        (reduce.at[0], reduce_v),
        (qkv.at[0], qkv_v),
        (proj.at[0], proj_v),
        (qkv_b, qkv_bv),
        (proj_b, proj_bv),
        (expand_b, expand_bv),
        (reduce_b, reduce_bv),
    ]
    moves += [(ref, gains_v.at[i]) for i, ref in enumerate((g1, s1, g2, s2))]
    copies = [pltpu.make_async_copy(a, b, sems.at[i]) for i, (a, b) in enumerate(moves)]
    for copy in copies:
        copy.start()
    weights[288:304, :] = jnp.zeros((16, 384), BF)
    lines[...] = jnp.zeros_like(lines)
    blank = jnp.zeros((HEADS, 256 - SIDE), F32)
    for copy in copies[:HEADS]:
        copy.wait()
    for zr in range(WZ * HALF):
        z, r = divmod(zr, HALF)
        for zk in range(WZ):
            start = ((z * WZ + zk) * HALF + r) * SIDE
            target = pl.ds(zr, HEADS, stride=8)
            lines[2 * zk, target, :] = table_v[0:HEADS, start : start + 128]
            tail = table_v[0:HEADS, start + 128 : start + SIDE]
            lines[2 * zk + 1, target, :] = jnp.concatenate([tail, blank], axis=1)
    for zk in range(WZ):
        whole = jnp.concatenate([lines[2 * zk], lines[2 * zk + 1]], axis=1)
        high = whole.astype(BF)
        rest = whole - high.astype(F32)
        middle = rest.astype(BF)
        low = (rest - middle.astype(F32)).astype(BF)
        for i, part in enumerate((high, middle, low)):
            rows = slice(288 + 144 * zk + 48 * i, 288 + 144 * zk + 48 * (i + 1))
            kept[rows, :] = part
            sent[rows, :] = part
    arrived = iter(copies[HEADS:])
    next(arrived).wait()
    kept[0:288, 0:C] = kept_v[...].reshape(288, C)
    next(arrived).wait()
    sent[0:288, 0:C] = sent_v[...].reshape(288, C)
    next(arrived).wait()
    weights[0:192, 192:384] = expand_v[...]
    next(arrived).wait()
    weights[192:288, 0:192] = reduce_v[0:96, :]
    weights[192:288, 192:384] = reduce_v[96:192, :]
    next(arrived).wait()
    weights[0:144, 0:192] = qkv_v[...]
    next(arrived).wait()
    weights[144:192, 0:192] = proj_v[...]
    for copy in arrived:
        copy.wait()
    weights[288:289, 0:144] = qkv_bv[...]
    weights[288:289, 144:192] = proj_bv[...]
    weights[288:289, 192:384] = expand_bv[...]
    weights[289:290, 0:48] = reduce_bv[...]
    for i in range(4):
        gains_out[i : i + 1, :] = gains_v[i].astype(F32)
    share[...] = weights[pl.ds(pl.multiple_of(144 * core, 16), 160), :]


def join_kernel(own, first, second, third, out):
    me = lax.axis_index("tp")
    out[me] = own[...]
    for k, ref in ((2, first), (3, second), (1, third)):
        out[lax.rem(me + 4 - k, 4)] = ref[...]


def norm(x, gain, shift):
    mean = jnp.sum(x, axis=-1, keepdims=True) * (1.0 / C)
    centred = x - mean
    var = jnp.sum(centred * centred, axis=-1, keepdims=True) * (1.0 / C)
    return centred * lax.rsqrt(var + EPS) * gain + shift


def dot(a, b):
    return jnp.dot(a, b, preferred_element_type=F32)


def dot_t(a, b):
    return lax.dot_general(a, b, (((1,), (1,)), ((), ())), preferred_element_type=F32)


def assemble(pack, wqkv, wproj, wexp, wred, bqkv, brow):
    for j in range(4):
        low, high = pack.at[0, j], pack.at[1, j]
        wqkv[144 * j : 144 * (j + 1), :] = low[0:144, 0:C]
        wproj[48 * j : 48 * (j + 1), :] = high[0:48, 0:C]
        wexp[0:144, C * j : C * (j + 1)] = low[0:144, C : 2 * C]
        wexp[144:192, C * j : C * (j + 1)] = high[0:48, C : 2 * C]
        wred[C * j : C * j + 96, :] = high[48:144, 0:C]
        wred[C * j + 96 : C * (j + 1), :] = high[48:144, C : 2 * C]
        brow[0:1, C * j : C * (j + 1)] = high[144:145, C : 2 * C].astype(F32)
        brow[1:2, 48 * j : 48 * (j + 1)] = high[144:145, 144:192].astype(F32)
        brow[2:3, 48 * j : 48 * (j + 1)] = high[145:146, 0:48].astype(F32)
        at = 144 * j
        while at < 144 * (j + 1):
            part, inner = divmod(at, C)
            size = min(C - inner, 144 * (j + 1) - at)
            source = at - 144 * j
            bqkv[part : part + 1, inner : inner + size] = high[
                144:145, source : source + size
            ].astype(F32)
            at += size


def expand_bias(fields, turn, bias):
    for half, field in enumerate(fields):
        parts = None
        for zk in range(WZ):
            rows = slice(288 + 144 * zk, 288 + 144 * (zk + 1))
            part = dot(field[rows, 0:SIDE], turn[SIDE * zk : SIDE * (zk + 1), :])
            parts = part if parts is None else parts + part
        turned = (parts[0:48] + parts[48:96] + parts[96:144]) * LOG2E
        for wq in range(WW):
            start = KEYS * (WW - 1 - wq)
            piece = turned[:, start : start + WIN]
            row = wq * KEYS + half * WZ * HALF
            for h in range(HEADS):
                bias[h, row : row + WZ * HALF, :] = piece[8 * h : 8 * h + WZ * HALF, :]


def attend(q, k, v, bias):
    head_of = lax.broadcasted_iota(jnp.int32, (WIN, C), 1) // DIM
    scale = LOG2E / float(np.sqrt(DIM))
    zero = jnp.zeros((WIN, C), BF)
    stacked = jnp.concatenate([jnp.where(head_of == h, q, zero) for h in range(HEADS)], axis=0)
    scores = dot_t(stacked, k)
    probs, inverse = [], []
    for h in range(HEADS):
        own = scores[WIN * h : WIN * (h + 1)] * scale + bias[h]
        weights = jnp.exp2(own - jnp.max(own, axis=-1, keepdims=True))
        inverse.append(1.0 / jnp.sum(weights, axis=-1, keepdims=True))
        probs.append(weights.astype(BF))
    values = dot(jnp.concatenate(probs, axis=0), v)
    total = values[0:WIN] * inverse[0]
    for h in range(1, HEADS):
        part = values[WIN * h : WIN * (h + 1)] * inverse[h]
        total = jnp.where(head_of == h, part, total)
    return total.astype(BF)


def block(x, gains, wqkv, wproj, wexp, wred, bqkv, brow, bias):
    floats = x.astype(F32)
    normed = norm(floats, gains[0:1, :], gains[1:2, :]).astype(BF)
    q, k, v = (
        (dot_t(normed, wqkv[C * i : C * (i + 1), :]) + bqkv[i : i + 1, :]).astype(BF)
        for i in range(3)
    )
    windows = (slice(at, at + WIN) for at in range(0, x.shape[0], WIN))
    attended = jnp.concatenate([attend(q[rows], k[rows], v[rows], bias) for rows in windows], axis=0)
    middle = (floats + dot_t(attended, wproj[...]) + brow[1:2, 0:C]).astype(BF)
    middle_floats = middle.astype(F32)
    normed_two = norm(middle_floats, gains[2:3, :], gains[3:4, :]).astype(BF)
    total = middle_floats + brow[2:3, 0:C]
    for at in range(0, MLP, 256):
        pre = dot(normed_two, wexp[:, at : at + 256]) + brow[0:1, at : at + 256]
        hidden = (0.5 * pre * (1.0 + lax.erf(pre * float(np.sqrt(0.5))))).astype(BF)
        total = total + dot(hidden, wred[at : at + 256, :])
    return total.astype(BF)


def daily_kernel(own, other, pick, pack, gains, turn, out_0, out_1, bias, *mats):
    assemble(pack, *mats)
    expand_bias((own, other), turn.at[lax.rem(lax.axis_index("lat"), 2)], bias)

    @pl.when(lax.axis_index("section") == 0)
    def _():
        tokens = []
        for t in range(2):
            rows = slice(WIN * t, WIN * (t + 1))
            source = jnp.concatenate([own[rows, 0:C], other[rows, 0:C]], axis=0)
            tokens.append(dot(pick[...], source).astype(BF))
        result = block(jnp.concatenate(tokens, axis=0), gains, *mats, bias)
        for w, (out, side) in enumerate(((out_0, 0), (out_0, C), (out_1, 0), (out_1, C))):
            out[:, side : side + C] = result[WIN * w : WIN * (w + 1)]


def chained_block(received, own, split, gains, bias, mats, hold):
    section = lax.axis_index("section")

    @pl.when(section == 0)
    def _():
        hold[0:WIN, :] = own[:, 0:C]
        hold[WIN : 2 * WIN, :] = own[:, C : 2 * C]

    @pl.when(section == 1)
    def _():
        x = jnp.concatenate([received[:, 0:C], received[:, C : 2 * C]], axis=0)
        hold[...] = block(x, gains, *mats, bias)

    ordered = dot(split[...], hold[...]).astype(BF)
    return ordered[0:WIN], ordered[WIN : 2 * WIN]


def chained_kernel(received, own, split, gains, bias, *rest):
    *mats, out, hold = rest
    out[0], out[1] = chained_block(received, own, split, gains, bias, mats, hold)


def last_kernel(earlier, received, own, split, gains, bias, *rest):
    *mats, out, hold = rest
    core = lax.rem(lax.axis_index("lat"), 2)
    out[core, 0] = earlier[0]
    out[1 - core, 0] = earlier[1]
    mine, theirs = chained_block(received, own, split, gains, bias, mats, hold)
    out[core, 1] = mine
    out[1 - core, 1] = theirs


def place_kernel(both, out, sems):
    core = lax.rem(lax.axis_index("lat"), 2)
    copies = [
        pltpu.make_async_copy(both.at[side, core], out.at[:, pl.ds(24 * side, 24), :], sems.at[side])
        for side in range(2)
    ]
    for copy in copies:
        copy.start()
    for copy in copies:
        copy.wait()


def call(kernel, out_shape, args, scratch=(), flops=0):
    many = isinstance(out_shape, tuple)
    return pl.pallas_call(
        kernel,
        out_shape=out_shape,
        in_specs=[VMEM] * len(args),
        out_specs=(VMEM,) * len(out_shape) if many else VMEM,
        scratch_shapes=list(scratch),
        compiler_params=PARAMS,
        cost_estimate=pl.CostEstimate(flops=flops, bytes_accessed=1 << 20, transcendentals=0),
    )(*args)


def on_device(
    initial_field,
    first_gain,
    first_shift,
    qkv_weight,
    qkv_bias,
    proj_weight,
    proj_bias,
    second_gain,
    second_shift,
    expand_weight,
    expand_bias_row,
    reduce_weight,
    reduce_bias,
    earth_bias,
):
    lat_count = lax.axis_size("lat")
    pairs = [[2 * i, 2 * i + 1] for i in range(lat_count // 2)]
    shape = jax.ShapeDtypeStruct
    hbm = pl.BlockSpec(memory_space=pltpu.HBM)
    operands = (
        jnp.swapaxes(qkv_weight, 1, 2),
        jnp.swapaxes(proj_weight, 1, 2),
        expand_weight,
        reduce_weight,
        qkv_bias,
        proj_bias,
        expand_bias_row,
        reduce_bias,
        initial_field.reshape(12, 48, C),
        earth_bias.reshape(HEADS, 1, -1),
        first_gain,
        first_shift,
        second_gain,
        second_shift,
    )
    pick = jnp.asarray(pick_rows())
    split = jnp.asarray(pick_rows().T)
    turn = jnp.asarray(turn_columns())
    share, kept, sent, gains = pl.pallas_call(
        load_kernel,
        out_shape=(
            shape((160, 2 * C), BF),
            shape((576, 256), BF),
            shape((576, 256), BF),
            shape((4, C), F32),
        ),
        in_specs=[hbm] * len(operands),
        out_specs=(VMEM,) * 4,
        scratch_shapes=[
            pltpu.VMEM((144, C), BF),
            pltpu.VMEM((48, C), BF),
            pltpu.VMEM((C, C), BF),
            pltpu.VMEM((C, C), BF),
            pltpu.VMEM((1, 144), BF),
            pltpu.VMEM((1, 48), BF),
            pltpu.VMEM((1, C), BF),
            pltpu.VMEM((1, 48), BF),
            pltpu.VMEM((12, 24, C), BF),
            pltpu.VMEM((12, 24, C), BF),
            pltpu.VMEM((8, 1656), F32),
            pltpu.VMEM((4, 1, C), BF),
            pltpu.VMEM((4, 48, 128), F32),
            pltpu.VMEM((304, 2 * C), BF),
            pltpu.SemaphoreType.DMA((20,)),
        ],
        compiler_params=PARAMS,
    )(*(pltpu.with_memory_space_constraint(x, pltpu.HBM) for x in operands))
    tp_count = lax.axis_size("tp")
    shares = [
        lax.ppermute(share, "tp", [(i, (i + k) % tp_count) for i in range(tp_count)]) for k in (2, 3, 1)
    ]
    swap = [(i, i ^ 1) for i in range(lat_count)]
    other = lax.ppermute(sent, "lat", swap)
    joined = call(join_kernel, shape((4, 160, 2 * C), BF), (share, *shares))
    pack = lax.all_gather(joined, "lat", axis_index_groups=pairs)
    mats = (
        shape((3 * C, C), BF),
        shape((C, C), BF),
        shape((C, MLP), BF),
        shape((MLP, C), BF),
        shape((3, C), F32),
        shape((3, MLP), F32),
    )
    flops = 2 * 576 * 192 * 192 * 14
    dense = shape((WIN, 2 * C), BF)
    daily_0, daily_1, bias, *mats = call(
        daily_kernel,
        (dense, dense, shape((HEADS, WIN, WIN), F32), *mats),
        (kept, other, pick, pack, gains, turn),
        flops=flops,
    )
    received_0 = lax.ppermute(daily_0, "section", [(0, 1)])
    received_1 = lax.ppermute(daily_1, "section", [(0, 1)])
    hold = [pltpu.VMEM((2 * WIN, C), BF)]
    shared = (split, gains, bias, *mats)
    earlier = call(
        chained_kernel,
        shape((2, WIN, C), BF),
        (received_0, daily_0, *shared),
        hold,
        flops // 2,
    )
    states = call(
        last_kernel,
        shape((2, 2, WIN, C), BF),
        (earlier, received_1, daily_1, *shared),
        hold,
        flops // 2,
    )
    both = lax.all_gather(states, "lat", axis_index_groups=pairs)
    placed = pl.pallas_call(
        place_kernel,
        out_shape=shape((12, 48, C), BF),
        in_specs=[pl.BlockSpec(memory_space=pl.ANY)],
        out_specs=pl.BlockSpec(memory_space=pl.ANY),
        scratch_shapes=[pltpu.SemaphoreType.DMA((2,))],
        compiler_params=PARAMS,
    )(both.reshape(2, 2, 12, 24, C))
    return placed.reshape(1, 2, 2, 3, 48, C)


def solution(mesh):
    return jax.shard_map(
        on_device,
        mesh=mesh,
        in_specs=(
            P(None, "tp", "lat", None, None),
            P("section", None),
            P("section", None),
            P("section", None, "tp"),
            P("section", "tp"),
            P("section", None, "tp"),
            P("section", "tp"),
            P("section", None),
            P("section", None),
            P("section", None, "tp"),
            P("section", "tp"),
            P("section", "tp", None),
            P("section", "tp"),
            P("section", "tp", "lat", None, None),
        ),
        out_specs=P("section", None, "tp", "lat", None, None),
        check_vma=False,
    )
```
